32 devices in a mesh: group: 2 (over y), head: 4 (over z), cache: 4 (over x, core).
Axes of the slice: x: 2, y: 2, z: 4, core: 2. Of those that a mesh axis runs over, the one named last changes fastest.
Arguments:
- queries: bfloat16 [512, 4096], P(('group', 'head')), parts along dimension 0, may hold values from -8 to 8
- keys: bfloat16 [256, 128, 4096], P(('group', 'cache'), None, 'head'), parts along dimension 0, may hold values from -8 to 8
- values: bfloat16 [256, 128, 4096], P(('group', 'cache'), None, 'head'), parts along dimension 0, may hold values from -6 to 6
- page_lists: int32 [8, 32], P(('group', 'cache')), parts along dimension 0, may hold values from 0 to 31, as said below
- page_counts: int32 [8], P(('group', 'cache')), parts along dimension 0, may hold values from 1 to 32, as said below
Outputs:
- attended: float32 [512, 4096], P(('group', 'head', 'cache')), parts along dimension 0
- log_sums: float32 [512, 32], P(('group', 'head', 'cache')), parts along dimension 0
The draws below stay inside these ranges and needn't reach their ends.
There are 2 independent parts, one for each index of `group`. The reference program is written for one: setup_inputs(seed, part) draws one part's arguments, and reference() takes and returns one part's arrays. A program takes and returns all parts, laid end to end along the dimension named above; each array names one. Nothing has to cross between parts.
Inputs may be any that keep to these rules, and one draw needn't show every extreme that they name: `page_lists`: row c holds 32 distinct page ids of owner c's pool; only its first page_counts[c] entries are attended. `page_counts`: some owner lists exactly 32 pages in every draw.
All inputs are finite; a program needn't handle non-finite values.
Results may differ from the reference program's by a relative error of at most 0.00038.
Values may be sent and summed in bfloat16 or wider, within the bound.
A program may use at most 64 MiB of HBM per device.

```python
import math
import jax
import jax.numpy as jnp
from jax import lax

HEADS = 32
DH = 128
PAGE = 128
POOL = 32
MOST = 32
Q_TOK = 256
OWNERS = 4


def page_tables(key):
    base = jax.random.fold_in(key, 101)
    owner_keys = jax.random.split(jax.random.fold_in(base, 1), OWNERS)
    listed = jax.vmap(lambda owner_key: jax.random.permutation(owner_key, POOL)[:MOST])(owner_keys).astype(jnp.int32)
    counts = jax.random.randint(jax.random.fold_in(base, 2), (OWNERS,), 1, MOST // 2 + 1)
    busiest = jax.random.randint(jax.random.fold_in(base, 3), (), 0, OWNERS)
    counts = jnp.where(jnp.arange(OWNERS) == busiest, MOST, counts).astype(jnp.int32)
    return (listed, counts)


def drawn_draw(key, shape):
    return jnp.clip(1.7 * jax.random.normal(key, shape, jnp.float32), -8.0, 8.0)


def draw_page_lists(key, part):
    listed, counts = page_tables(key)
    return listed


def draw_page_counts(key, part):
    listed, counts = page_tables(key)
    return counts


def draw_queries(key, part):
    shape = (Q_TOK, HEADS * DH)
    drawn = drawn_draw(jax.random.fold_in(key, 304), shape)
    return drawn.astype(jnp.bfloat16)


def draw_keys(key, part):
    shape = (OWNERS * POOL, PAGE, HEADS * DH)
    drawn = drawn_draw(jax.random.fold_in(key, 405), shape)
    return drawn.astype(jnp.bfloat16)


def block_levels(stream_key, shape, cuts, smallest, largest):
    factor_of, own = 1.0, jax.random.fold_in(stream_key, 6)
    for position, blocks in cuts:
        steps = jnp.exp(jax.random.uniform(jax.random.fold_in(own, position), (blocks,), jnp.float32, smallest / len(cuts), largest / len(cuts)))
        factor_of = factor_of * jnp.repeat(steps, shape[position] // blocks).reshape([-1 if axis == position else 1 for axis in range(len(shape))])
    return factor_of


def scatter_about(key, dims, scale, most, shards=(), kind=jnp.bfloat16):
    result = scale * jax.random.normal(key, dims, jnp.float32)
    if shards:
        result = result * block_levels(key, dims, shards, -0.22, 0.18)
    return jnp.clip(result, -most, most).astype(kind)


def setup_inputs(seed: int = 0, part: int = 0) -> dict:
    arg_keys = jax.random.split(jax.random.key(seed), 6)
    part_keys = jax.random.split(jax.random.fold_in(arg_keys[5], part), 6)
    queries = draw_queries(jax.random.fold_in(jax.random.fold_in(arg_keys[5], part), 71), part)
    keys = draw_keys(jax.random.fold_in(jax.random.fold_in(arg_keys[5], part), 71), part)
    values = scatter_about(part_keys[2], (OWNERS * POOL, PAGE, HEADS * DH), 1.0, 6.0, ((0, 4), (2, 4)))
    page_lists = draw_page_lists(jax.random.fold_in(jax.random.fold_in(arg_keys[5], part), 71), part)
    page_counts = draw_page_counts(jax.random.fold_in(jax.random.fold_in(arg_keys[5], part), 71), part)
    return {"queries": queries, "keys": keys, "values": values, "page_lists": page_lists, "page_counts": page_counts}


lowest = -1e+30

def reference(queries, keys, values, page_lists, page_counts):
    score_scale = 1.0 / math.sqrt(DH)
    query_heads = queries.reshape(Q_TOK, HEADS, DH).astype(jnp.float32)
    owner_ids = jnp.arange(OWNERS, dtype=jnp.int32)
    page_rows = (owner_ids[:, None] * POOL + page_lists).reshape(-1).astype(jnp.int32)
    live = (jnp.arange(MOST, dtype=jnp.int32)[None, :] < page_counts[:, None]).reshape(-1)

    def update(state, row):
        best, total, accum = state
        key_page = lax.dynamic_index_in_dim(keys, row, 0, keepdims=False).reshape(PAGE, HEADS, DH).astype(jnp.float32)
        value_page = lax.dynamic_index_in_dim(values, row, 0, keepdims=False).reshape(PAGE, HEADS, DH).astype(jnp.float32)
        scores = jnp.einsum('thd,khd->thk', query_heads, key_page) * score_scale
        page_max = lax.optimization_barrier(jnp.max(scores, axis=-1))
        rounded = jnp.exp(scores - page_max[..., None]).astype(jnp.bfloat16)
        weights = lax.optimization_barrier(rounded).astype(jnp.float32)
        page_sum = lax.optimization_barrier(jnp.sum(weights, axis=-1))
        page_out = jnp.einsum('thk,khd->thd', weights, value_page)
        running = jnp.maximum(best, page_max)
        keep = jnp.exp(best - running)
        fresh = jnp.exp(page_max - running)
        return (running, total * keep + fresh * page_sum, accum * keep[..., None] + fresh[..., None] * page_out)

    def visit(state, item):
        row, used = item
        return (lax.cond(used, lambda inner: update(inner, row), lambda inner: inner, state), None)
    start = (jnp.full((Q_TOK, HEADS), lowest, jnp.float32), jnp.zeros((Q_TOK, HEADS), jnp.float32), jnp.zeros((Q_TOK, HEADS, DH), jnp.float32))
    (best, total, accum), _ = lax.scan(visit, start, (page_rows, live))
    attended = (accum / total[..., None]).reshape(Q_TOK, HEADS * DH)
    log_sums = best + jnp.log(total)
    return (attended, log_sums)
```

```python
import functools
import math

import jax
import jax.numpy as jnp
from jax import lax
from jax.experimental import pallas as pl
from jax.experimental.pallas import tpu as pltpu
from jax.sharding import PartitionSpec as P

DH = 128
PAGE = 128
LANES = 128
TILE = 256
ROWS = DH + 8
PAIR = 2
JOIN = 4
BLOCK = 16
PREFETCH = 2
SCALE = 1.0 / math.sqrt(DH)
LOG2_SCALE = SCALE * math.log2(math.e)

lowest = -1e30
highest = 3e38


def attend(query, k_ref, v_ref, caps, pages, acc, scores, turned):
    scaled = query * LOG2_SCALE
    high = scaled.astype(jnp.bfloat16)
    low = (scaled - high.astype(jnp.float32)).astype(jnp.bfloat16)
    turned[...] = jnp.concatenate([high, low], axis=1).T
    acc[...] = jnp.zeros_like(acc)
    ones = jnp.ones((16, PAIR * PAGE), jnp.bfloat16)
    block = min(BLOCK, pages)
    blocks = pages // block

    def score(index):
        rows = k_ref[index * block:(index + 1) * block].reshape(block * PAGE, DH)
        scores[index % 2] = jnp.dot(
            jnp.concatenate([rows, rows], axis=1), turned[...], preferred_element_type=jnp.float32
        ).reshape(block, PAGE, TILE)

    def weigh(index, at):
        page = index * block + at
        limits = [caps[page + i:page + i + 1, :] for i in range(PAIR)]
        top = functools.reduce(jnp.maximum, [
            jnp.minimum(jnp.max(scores[index % 2, at + i], axis=0, keepdims=True), limits[i]) for i in range(PAIR)
        ])
        weights = jnp.concatenate([
            jnp.exp2(scores[index % 2, at + i] - jnp.maximum(top, -limits[i])).astype(jnp.bfloat16)
            for i in range(PAIR)
        ], axis=0)
        left = jnp.concatenate([v_ref[page:page + PAIR].reshape(PAIR * PAGE, DH).T, ones], axis=0)
        return top, jnp.dot(left, weights, preferred_element_type=jnp.float32)[:ROWS]

    score(0)
    best = jnp.full((1, TILE), lowest, jnp.float32)
    for index in range(blocks):
        if index + 1 < blocks:
            score(index + 1)
        waiting = []
        for at in range(0, block, PAIR):
            waiting.append(weigh(index, at))
            if len(waiting) == JOIN or at + PAIR >= block:
                running = functools.reduce(jnp.maximum, [top for top, _ in waiting], best)
                joined = acc[...] * jnp.exp2(best - running)
                for top, out in waiting:
                    joined += out * jnp.exp2(top - running)
                acc[...] = joined
                best, waiting = running, []
    return best


def kernel(
    plan, q_hbm, k_hbm, v_hbm, lists_hbm, counts_hbm, out_ref, log_ref,
    lists, counts, caps, k_buf, v_buf, q_all, acc, scores, turned, part, part_in, cross_out, cross_in, piece_out, log_rows, log_out, log_in,
    lists_sem, counts_sem, k_sem, v_sem, own_sem, q_send, q_recv, pass_send, pass_recv,
    part_send, part_recv, cross_send, cross_recv, piece_send, piece_recv, log_send, log_recv,
):
    heads, tiles, sources, n_head, n_cache, cuts = plan
    batches = len(cuts) - 1
    groups = heads * tiles
    n_cross = n_cache // 2
    pages = k_hbm.shape[0]
    half = q_hbm.shape[0] // 2
    share = q_hbm.shape[0] // n_cache
    chunk = LANES // n_cross
    depth = DH // n_cross
    me = lax.axis_index("head")
    seat = lax.axis_index("cache")
    core = lax.rem(seat, 2)
    line = seat // 2
    sibling = seat + 1 - 2 * core

    def peer_of(index, count, offset):
        return lax.rem(index + offset, count)

    def load(head):
        columns = pl.ds(pl.multiple_of(head * DH, DH), DH)
        return (
            pltpu.make_async_copy(k_hbm.at[:, :, columns], k_buf.at[head], k_sem.at[head]),
            pltpu.make_async_copy(v_hbm.at[:, :, columns], v_buf.at[head], v_sem.at[head]),
        )

    def width_of(batch):
        return slice(cuts[batch] * DH, cuts[batch + 1] * DH)

    def query_source(batch, owner):
        rows = pl.ds(pl.multiple_of(core * half, half), half)
        start = pl.multiple_of((owner * heads + cuts[batch]) * DH, DH)
        return q_hbm.at[rows, pl.ds(start, (cuts[batch + 1] - cuts[batch]) * DH)]

    def own_query(batch):
        return pltpu.make_async_copy(
            query_source(batch, me), q_all.at[core, me, :, width_of(batch)], own_sem.at[batch]
        )

    def query_copy(batch, offset, source):
        peer = peer_of(me, n_head, offset)
        return pltpu.make_async_remote_copy(
            src_ref=query_source(batch, peer), dst_ref=q_all.at[core, source, :, width_of(batch)],
            send_sem=q_send.at[batch, offset - 1], recv_sem=q_recv.at[batch, source],
            device_id={"head": peer}, device_id_type=pl.DeviceIdType.MESH,
        )

    def pass_copy(batch, side):
        return pltpu.make_async_remote_copy(
            src_ref=q_all.at[side, :, :, width_of(batch)], dst_ref=q_all.at[side, :, :, width_of(batch)],
            send_sem=pass_send.at[batch], recv_sem=pass_recv.at[batch],
            device_id={"cache": sibling}, device_id_type=pl.DeviceIdType.MESH,
        )

    def part_copy(group):
        return pltpu.make_async_remote_copy(
            src_ref=part.at[group, 1 - core], dst_ref=part_in.at[group],
            send_sem=part_send.at[group], recv_sem=part_recv.at[group],
            device_id={"cache": sibling}, device_id_type=pl.DeviceIdType.MESH,
        )

    def cross_copy(group, offset, source):
        peer = peer_of(line, n_cross, offset)
        return pltpu.make_async_remote_copy(
            src_ref=cross_out.at[group, peer], dst_ref=cross_in.at[group, source],
            send_sem=cross_send.at[group, offset - 1], recv_sem=cross_recv.at[group, source],
            device_id={"cache": peer * 2 + core}, device_id_type=pl.DeviceIdType.MESH,
        )

    def columns_of(source, head):
        return pl.ds(pl.multiple_of((source * heads + head) * DH, DH), DH)

    def piece_copy(group, place, source, target):
        head = group // tiles
        return pltpu.make_async_remote_copy(
            src_ref=piece_out.at[group, place], dst_ref=out_ref.at[:, columns_of(source, head)],
            send_sem=piece_send.at[group, place], recv_sem=piece_recv.at[head, source],
            device_id={"head": target}, device_id_type=pl.DeviceIdType.MESH,
        )

    def log_copy(offset, source):
        peer = peer_of(me, n_head, offset)
        return pltpu.make_async_remote_copy(
            src_ref=log_out.at[peer], dst_ref=log_in.at[source],
            send_sem=log_send.at[offset - 1], recv_sem=log_recv.at[source],
            device_id={"head": peer}, device_id_type=pl.DeviceIdType.MESH,
        )

    barrier = pltpu.get_barrier_semaphore()
    for offset in range(1, n_head):
        pl.semaphore_signal(
            barrier, inc=1, device_id={"head": peer_of(me, n_head, offset)},
            device_id_type=pl.DeviceIdType.MESH,
        )
    pl.semaphore_signal(barrier, inc=1, device_id={"cache": sibling}, device_id_type=pl.DeviceIdType.MESH)
    for offset in range(1, n_cross):
        pl.semaphore_signal(
            barrier, inc=1, device_id={"cache": peer_of(line, n_cross, offset) * 2 + core},
            device_id_type=pl.DeviceIdType.MESH,
        )
    for batch in range(batches):
        own_query(batch).start()
    pl.semaphore_wait(barrier, n_head + n_cross - 1)
    for batch in range(batches):
        for offset in range(1, n_head):
            query_copy(batch, offset, me).start()
    lists_copy = pltpu.make_async_copy(lists_hbm, lists, lists_sem)
    counts_copy = pltpu.make_async_copy(counts_hbm, counts, counts_sem)
    lists_copy.start()
    counts_copy.start()
    for head in range(min(PREFETCH, heads)):
        for copy in load(head):
            copy.start()
    log_rows[...] = jnp.zeros_like(log_rows)
    lists_copy.wait()
    counts_copy.wait()
    slots = lists.shape[1]
    used = lax.broadcasted_iota(jnp.int32, (1, slots), 1) < counts[0]
    listed = jnp.where(used, lists[...], -1)
    match = listed == lax.broadcasted_iota(jnp.int32, (pages, slots), 0)
    cap = jnp.max(jnp.where(match, highest, lowest), axis=1, keepdims=True)
    caps[...] = jnp.broadcast_to(cap, caps.shape)

    def hand_on(batch):
        own_query(batch).wait()
        for offset in range(1, n_head):
            query_copy(batch, offset, peer_of(me, n_head, offset)).wait_recv()
        pass_copy(batch, core).start()

    def only_if(condition, action):
        if isinstance(condition, bool):
            if condition:
                action()
        else:
            pl.when(condition)(action)

    def compute(group):
        head = group // tiles
        tile = lax.rem(group, tiles)
        first = tiles == 1 or tile == 0

        def ready():
            for batch in range(batches):
                only_if(head == cuts[batch], lambda: pass_copy(batch, 1 - core).wait_recv())
            for copy in load(head):
                copy.wait()
            if heads > PREFETCH:
                @pl.when(head + PREFETCH < heads)
                def _():
                    for copy in load(head + PREFETCH):
                        copy.start()
            for batch in range(2, batches):
                pl.when(head == cuts[batch] - 1)(lambda: hand_on(batch))

        only_if(first, ready)
        members = [2 * x + side for side in range(2) for x in range(n_cross)]
        pieces = []
        for member in members:
            side, at = divmod(member * share, half)
            for l in range(sources):
                rows = q_all[side, tile * sources + l, :, pl.ds(pl.multiple_of(head * DH, DH), DH)]
                pieces.append(rows[at:at + share].astype(jnp.float32))
        query = jnp.concatenate(pieces, axis=0)

        best = attend(query, k_buf.at[head], v_buf.at[head], caps, pages, acc, scores, turned)
        row = lax.broadcasted_iota(jnp.int32, (8, TILE), 0)
        tail = jnp.where(row == 1, best, acc[DH:ROWS])
        for side in range(2):
            lanes = slice(side * LANES, (side + 1) * LANES)
            part[group, side, :DH] = acc[:DH, lanes]
            part[group, side, DH:ROWS] = tail[:, lanes]
        part_copy(group).start()

    def merge(group):
        part_copy(group).wait_recv()
        totals = [part[group, core, DH:DH + 1], part_in[group, DH:DH + 1]]
        bests = [part[group, core, DH + 1:DH + 2], part_in[group, DH + 1:DH + 2]]
        top = jnp.maximum(*bests)
        keeps = [jnp.exp2(best - top) for best in bests]
        total = totals[0] * keeps[0] + totals[1] * keeps[1]
        result = part[group, core, :DH] * keeps[0] + part_in[group, :DH] * keeps[1]
        row = lax.broadcasted_iota(jnp.int32, (8, LANES), 0)
        tail = jnp.where(row == 1, top, total)
        for x in range(n_cross):
            lanes = slice(x * chunk, (x + 1) * chunk)
            cross_out[group, x, :depth] = jnp.concatenate(
                [result[i * depth:(i + 1) * depth, lanes] for i in range(n_cross)], axis=1
            )
            cross_out[group, x, depth:] = jnp.concatenate([tail[:, lanes]] * n_cross, axis=1)
        for offset in range(1, n_cross):
            cross_copy(group, offset, line).start()
        cross_in[group, line] = cross_out[group, line]

    def finish(group):
        head = group // tiles
        tile = lax.rem(group, tiles)
        for offset in range(1, n_cross):
            cross_copy(group, offset, peer_of(line, n_cross, offset)).wait_recv()
        totals = [cross_in[group, x, depth:depth + 1] for x in range(n_cross)]
        bests = [cross_in[group, x, depth + 1:depth + 2] for x in range(n_cross)]
        top = functools.reduce(jnp.maximum, bests)
        keeps = [jnp.exp2(best - top) for best in bests]
        total = functools.reduce(jnp.add, [t * keep for t, keep in zip(totals, keeps)])
        inverse = 1.0 / total
        result = functools.reduce(
            jnp.add, [cross_in[group, x, :depth] * (keep * inverse) for x, keep in enumerate(keeps)]
        ).T
        log_rows[tile, pl.ds(me * heads + head, 1)] = top * math.log(2.0) + jnp.log(total)
        for l in range(sources):
            at = l * share
            piece_out[group, l] = jnp.concatenate(
                [result[i * chunk + at:i * chunk + at + share] for i in range(n_cross)], axis=1
            )
        send(group)

    def send(group):
        if tiles == 1:
            for offset in range(1, n_head):
                target = peer_of(me, n_head, offset)
                piece_copy(group, target, me, target).start()
            out_ref[:, columns_of(me, group)] = piece_out[group, me]
        else:
            for place in range(sources):
                target = lax.rem(group, tiles) * sources + place
                pl.when(target != me)(piece_copy(group, place, me, target).start)

                @pl.when(target == me)
                def _():
                    out_ref[:, columns_of(me, group // tiles)] = piece_out[group, place]

    def sent(group):
        if tiles == 1:
            for offset in range(1, n_head):
                target = peer_of(me, n_head, offset)
                piece_copy(group, target, me, target).wait_send()
        else:
            for place in range(sources):
                target = group % tiles * sources + place
                pl.when(target != me)(piece_copy(group, place, me, target).wait_send)

    for batch in range(min(2, batches)):
        hand_on(batch)

    def step(group, carry):
        compute(group)
        pl.when(group > 0)(lambda: merge(group - 1))
        pl.when(group > 2)(lambda: finish(group - 3))
        return carry

    lax.fori_loop(0, groups, step, 0)
    if groups > 2:
        finish(groups - 3)
    merge(groups - 1)
    for group in range(max(groups - 2, 0), groups):
        finish(group)
    for tile in range(tiles):
        columns = log_rows[tile].T
        for l in range(sources):
            log_out[tile * sources + l] = columns[l * share:(l + 1) * share]
    for offset in range(1, n_head):
        log_copy(offset, me).start()
    log_in[me] = log_out[me]
    for batch in range(batches):
        pass_copy(batch, core).wait_send()
        for offset in range(1, n_head):
            query_copy(batch, offset, me).wait_send()
    for group in range(groups):
        part_copy(group).wait_send()
        for offset in range(1, n_cross):
            cross_copy(group, offset, line).wait_send()
        sent(group)
    for head in range(heads):
        for offset in range(1, n_head):
            source = peer_of(me, n_head, offset)
            piece_copy(head * tiles, 0, source, source).wait_recv()
    for offset in range(1, n_head):
        log_copy(offset, me).wait_send()
    for offset in range(1, n_head):
        log_copy(offset, peer_of(me, n_head, offset)).wait_recv()
    log_ref[...] = functools.reduce(jnp.add, [log_in[s] for s in range(n_head)])[:, :log_ref.shape[1]]


def on_device(queries, keys, values, page_lists, page_counts):
    n_head = lax.axis_size("head")
    n_cache = lax.axis_size("cache")
    tok_local = queries.shape[0]
    heads = keys.shape[2] // DH
    pages = keys.shape[0]
    share = tok_local // n_cache
    sources = TILE // tok_local
    tiles = n_head // sources
    groups = heads * tiles
    n_cross = n_cache // 2
    depth = DH // n_cross
    cuts = tuple(sorted({0, min(1, heads), min(2, heads), min(4, heads), heads}))
    batches = len(cuts) - 1
    plan = (heads, tiles, sources, n_head, n_cache, cuts)
    dma = pltpu.SemaphoreType.DMA
    anywhere = pl.BlockSpec(memory_space=pl.ANY)
    attended, logged = pl.pallas_call(
        functools.partial(kernel, plan),
        out_shape=(
            pltpu.VMEM((share, queries.shape[1]), jnp.float32),
            pltpu.VMEM((share, n_head * heads), jnp.float32),
        ),
        in_specs=[anywhere] * 5,
        out_specs=(pl.BlockSpec(memory_space=pltpu.VMEM), pl.BlockSpec(memory_space=pltpu.VMEM)),
        scratch_shapes=[
            pltpu.VMEM(page_lists.shape, jnp.int32),
            pltpu.SMEM(page_counts.shape, jnp.int32),
            pltpu.VMEM((pages, TILE), jnp.float32),
            pltpu.VMEM((heads, pages, PAGE, DH), jnp.bfloat16),
            pltpu.VMEM((heads, pages, PAGE, DH), jnp.bfloat16),
            pltpu.VMEM((2, n_head, tok_local // 2, heads * DH), jnp.bfloat16),
            pltpu.VMEM((ROWS, TILE), jnp.float32),
            pltpu.VMEM((2, min(BLOCK, pages), PAGE, TILE), jnp.float32),
            pltpu.VMEM((2 * DH, TILE), jnp.bfloat16),
            pltpu.VMEM((groups, 2, ROWS, LANES), jnp.float32),
            pltpu.VMEM((groups, ROWS, LANES), jnp.float32),
            pltpu.VMEM((groups, n_cross, depth + 8, LANES), jnp.float32),
            pltpu.VMEM((groups, n_cross, depth + 8, LANES), jnp.float32),
            pltpu.VMEM((groups, sources, share, DH), jnp.float32),
            pltpu.VMEM((tiles, LANES, LANES), jnp.float32),
            pltpu.VMEM((n_head, share, LANES), jnp.float32),
            pltpu.VMEM((n_head, share, LANES), jnp.float32),
            dma(()),
            dma(()),
            dma((heads,)),
            dma((heads,)),
            dma((batches,)),
            dma((batches, n_head - 1)),
            dma((batches, n_head)),
            dma((batches,)),
            dma((batches,)),
            dma((groups,)),
            dma((groups,)),
            dma((groups, n_cross - 1)),
            dma((groups, n_cross)),
            dma((groups, sources)),
            dma((heads, n_head)),
            dma((n_head - 1,)),
            dma((n_head,)),
        ],
        compiler_params=pltpu.CompilerParams(
            collective_id=0, has_side_effects=True, vmem_limit_bytes=56 * 1024 * 1024
        ),
    )(queries, keys, values, page_lists, page_counts)
    return attended, logged


def solution(mesh):
    in_specs = (
        P(("group", "head"), None),
        P(("group", "cache"), None, "head"),
        P(("group", "cache"), None, "head"),
        P(("group", "cache"), None),
        P(("group", "cache")),
    )
    out_specs = (P(("group", "head", "cache"), None), P(("group", "head", "cache"), None))
    return jax.shard_map(
        on_device, mesh=mesh, in_specs=in_specs, out_specs=out_specs, check_vma=False
    )
```

```python
import functools
import math

import jax
import jax.numpy as jnp
from jax import lax
from jax.experimental import pallas as pl
from jax.experimental.pallas import tpu as pltpu
from jax.sharding import PartitionSpec as P

DH = 128
PAGE = 128
LANES = 128
TILE = 256
ROWS = DH + 8
PAIR = 2
JOIN = 4
BLOCK = 16
PREFETCH = 2
SCALE = 1.0 / math.sqrt(DH)
LOG2_E = math.log2(math.e)
LN_2 = math.log(2.0)
LOG2_SCALE = SCALE * LOG2_E

lowest = -1e30
highest = 3e38


def attend(query, k_ref, v_ref, caps, pages, acc, scores, turned):
    scaled = query * LOG2_SCALE
    high = scaled.astype(jnp.bfloat16)
    low = (scaled - high.astype(jnp.float32)).astype(jnp.bfloat16)
    turned[...] = jnp.concatenate([high, low], axis=1).T
    acc[...] = jnp.zeros_like(acc)
    ones = jnp.ones((16, PAIR * PAGE), jnp.bfloat16)
    block = min(BLOCK, pages)
    blocks = pages // block

    def score(index):
        rows = k_ref[index * block:(index + 1) * block].reshape(block * PAGE, DH)
        scores[index % 2] = jnp.dot(
            jnp.concatenate([rows, rows], axis=1), turned[...], preferred_element_type=jnp.float32
        ).reshape(block, PAGE, TILE)

    def weigh(index, at):
        page = index * block + at
        limits = [caps[page + i:page + i + 1, :] for i in range(PAIR)]
        top = functools.reduce(jnp.maximum, [
            jnp.minimum(jnp.max(scores[index % 2, at + i], axis=0, keepdims=True), limits[i]) for i in range(PAIR)
        ])
        weights = jnp.concatenate([
            jnp.exp2(scores[index % 2, at + i] - jnp.maximum(top, -limits[i])).astype(jnp.bfloat16)
            for i in range(PAIR)
        ], axis=0)
        left = jnp.concatenate([v_ref[page:page + PAIR].reshape(PAIR * PAGE, DH).T, ones], axis=0)
        return top, jnp.dot(left, weights, preferred_element_type=jnp.float32)[:ROWS]

    score(0)
    best = jnp.full((1, TILE), lowest, jnp.float32)
    for index in range(blocks):
        if index + 1 < blocks:
            score(index + 1)
        waiting = []
        for at in range(0, block, PAIR):
            waiting.append(weigh(index, at))
            if len(waiting) == JOIN or at + PAIR >= block:
                running = functools.reduce(jnp.maximum, [top for top, _ in waiting], best)
                joined = acc[...] * jnp.exp2(best - running)
                for top, out in waiting:
                    joined += out * jnp.exp2(top - running)
                acc[...] = joined
                best, waiting = running, []
    return best


def kernel(
    plan, q_hbm, k_hbm, v_hbm, lists_hbm, counts_hbm, out_ref, log_ref,
    lists, counts, caps, kv_buf, q_all, acc, scores, turned, part, part_in, piece_out, piece_in, log_out, log_in,
    lists_sem, counts_sem, kv_sem, own_sem, q_send, q_recv, pass_send, pass_recv,
    part_send, part_recv, piece_send, piece_recv, log_send, log_recv,
):
    heads, tiles, sources, n_head, n_cache, cuts = plan
    batches = len(cuts) - 1
    groups = heads * tiles
    n_cross = n_cache // 2
    others = n_head * n_cross - 1
    spots = n_cross * sources
    pages = k_hbm.shape[0]
    half = q_hbm.shape[0] // 2
    share = q_hbm.shape[0] // n_cache
    me = lax.axis_index("head")
    seat = lax.axis_index("cache")
    core = lax.rem(seat, 2)
    line = seat // 2
    sibling = seat + 1 - 2 * core
    place = line * n_head + me
    away = [(dx, dz) for dx in range(n_cross) for dz in range(n_head) if dx or dz]

    def peer_of(index, count, offset):
        return lax.rem(index + offset, count)

    def seat_of(x):
        return x * 2 + core

    def load(head):
        columns = pl.ds(pl.multiple_of(head * DH, DH), DH)
        sem = kv_sem.at[lax.rem(head, PREFETCH)]
        pltpu.make_async_copy(k_hbm.at[:, :, columns], kv_buf.at[head, 0], sem).start()
        pltpu.make_async_copy(v_hbm.at[:, :, columns], kv_buf.at[head, 1], sem).start()

    def wait_for(ref, sem):
        pltpu.make_async_copy(ref, ref, sem).wait()

    def width_of(batch):
        return slice(cuts[batch] * DH, cuts[batch + 1] * DH)

    def rows_of(batch, side):
        if batch == 0:
            return pl.ds(0, 2 * half)
        return pl.ds(pl.multiple_of(side * half, half), half)

    def query_source(first, last, owner):
        columns = pl.ds(pl.multiple_of((owner * heads + cuts[first]) * DH, DH), (cuts[last] - cuts[first]) * DH)
        return q_hbm.at[rows_of(first, core), columns]

    def own_copy(first, last):
        return pltpu.make_async_copy(
            query_source(first, last, me),
            q_all.at[me, rows_of(first, core), slice(cuts[first] * DH, cuts[last] * DH)], own_sem.at[min(first, 1)],
        )

    def send_queries(batch):
        for offset in range(1, n_head):
            peer = peer_of(me, n_head, offset)
            pltpu.make_async_remote_copy(
                src_ref=query_source(batch, batch + 1, peer),
                dst_ref=q_all.at[me, rows_of(batch, core), width_of(batch)],
                send_sem=q_send, recv_sem=q_recv.at[batch],
                device_id={"head": peer}, device_id_type=pl.DeviceIdType.MESH,
            ).start()

    def pass_copy(batch, side):
        return pltpu.make_async_remote_copy(
            src_ref=q_all.at[:, rows_of(batch, side), width_of(batch)],
            dst_ref=q_all.at[:, rows_of(batch, side), width_of(batch)],
            send_sem=pass_send, recv_sem=pass_recv.at[batch],
            device_id={"cache": sibling}, device_id_type=pl.DeviceIdType.MESH,
        )

    def arrive(batch):
        wait_for(q_all.at[pl.ds(0, n_head - 1), rows_of(batch, 0), width_of(batch)], q_recv.at[batch])

    def hand_on(batch):
        arrive(batch)
        pass_copy(batch, core).start()

    def part_copy(group):
        return pltpu.make_async_remote_copy(
            src_ref=part.at[group, 1 - core], dst_ref=part_in.at[group],
            send_sem=part_send, recv_sem=part_recv.at[group],
            device_id={"cache": sibling}, device_id_type=pl.DeviceIdType.MESH,
        )

    def piece_copy(group, x, z):
        return pltpu.make_async_remote_copy(
            src_ref=piece_out.at[group, x, lax.rem(z, sources)], dst_ref=piece_in.at[place, group // tiles],
            send_sem=piece_send, recv_sem=piece_recv,
            device_id={"head": z, "cache": seat_of(x)}, device_id_type=pl.DeviceIdType.MESH,
        )

    barrier = pltpu.get_barrier_semaphore()
    for dx, dz in away:
        pl.semaphore_signal(
            barrier, inc=1,
            device_id={"head": peer_of(me, n_head, dz), "cache": seat_of(peer_of(line, n_cross, dx))},
            device_id_type=pl.DeviceIdType.MESH,
        )
    pl.semaphore_signal(barrier, inc=1, device_id={"cache": sibling}, device_id_type=pl.DeviceIdType.MESH)
    own_copies = [own_copy(0, 1)] + ([own_copy(1, batches)] if batches > 1 else [])
    for copy in own_copies:
        copy.start()
    lists_copy = pltpu.make_async_copy(lists_hbm, lists, lists_sem)
    counts_copy = pltpu.make_async_copy(counts_hbm, counts, counts_sem)
    lists_copy.start()
    counts_copy.start()
    pl.semaphore_wait(barrier, others + 1)
    for batch in range(min(3, batches)):
        send_queries(batch)
    load(0)
    log_out[...] = jnp.zeros_like(log_out)
    lists_copy.wait()
    counts_copy.wait()
    slots = lists.shape[1]
    used = lax.broadcasted_iota(jnp.int32, (1, slots), 1) < counts[0]
    listed = jnp.where(used, lists[...], -1)
    match = listed == lax.broadcasted_iota(jnp.int32, (pages, slots), 0)
    cap = jnp.max(jnp.where(match, highest, lowest), axis=1, keepdims=True)
    caps[...] = jnp.broadcast_to(cap, caps.shape)
    for copy in own_copies:
        copy.wait()
    for head in range(1, min(PREFETCH, heads)):
        load(head)
    arrive(0)
    for batch in range(3, batches):
        send_queries(batch)
    if batches > 1:
        hand_on(1)

    def only_if(condition, action):
        if isinstance(condition, bool):
            if condition:
                action()
        else:
            pl.when(condition)(action)

    def compute(group):
        head = group // tiles
        tile = lax.rem(group, tiles)

        def ready():
            for batch in range(1, batches):
                pl.when(head == cuts[batch])(lambda: pass_copy(batch, 1 - core).wait_recv())
            wait_for(kv_buf.at[head], kv_sem.at[lax.rem(head, PREFETCH)])
            if heads > PREFETCH:
                pl.when(head + PREFETCH < heads)(lambda: load(head + PREFETCH))
            for batch in range(2, batches):
                pl.when(head == cuts[batch] - 1)(lambda: hand_on(batch))

        only_if(tiles == 1 or tile == 0, ready)
        members = [2 * x + side for side in range(2) for x in range(n_cross)]
        pieces = []
        for member in members:
            for l in range(sources):
                rows = q_all[tile * sources + l, :, pl.ds(pl.multiple_of(head * DH, DH), DH)]
                pieces.append(rows[member * share:(member + 1) * share].astype(jnp.float32))
        query = jnp.concatenate(pieces, axis=0)
        best = attend(query, kv_buf.at[head, 0], kv_buf.at[head, 1], caps, pages, acc, scores, turned)
        row = lax.broadcasted_iota(jnp.int32, (8, TILE), 0)
        tail = jnp.where(row == 1, best, acc[DH:ROWS])
        for side in range(2):
            lanes = slice(side * LANES, (side + 1) * LANES)
            part[group, side, :DH] = acc[:DH, lanes]
            part[group, side, DH:ROWS] = tail[:, lanes]
        part_copy(group).start()

    def merge(group):
        head = group // tiles
        tile = lax.rem(group, tiles)
        part_copy(group).wait_recv()
        totals = [part[group, core, DH:DH + 1], part_in[group, DH:DH + 1]]
        bests = [part[group, core, DH + 1:DH + 2], part_in[group, DH + 1:DH + 2]]
        top = jnp.maximum(*bests)
        keeps = [jnp.exp2(best - top) for best in bests]
        total = totals[0] * keeps[0] + totals[1] * keeps[1]
        inverse = 1.0 / total
        result = part[group, core, :DH] * (keeps[0] * inverse) + part_in[group, :DH] * (keeps[1] * inverse)
        level = jnp.broadcast_to(top + jnp.log(total) * LOG2_E, (spots, LANES))
        level = pltpu.roll(level, 0, 1, stride=share, stride_axis=0)
        level = pltpu.roll(level, lax.rem((head + 1) * share, LANES), 1)
        lane = lax.broadcasted_iota(jnp.int32, (spots, LANES), 1)
        chosen = jnp.logical_and(lane >= head * share, lane < (head + 1) * share)
        log_out[tile] = jnp.where(chosen, level, log_out[tile])
        rows = result.T
        for x in range(n_cross):
            for l in range(sources):
                at = (x * sources + l) * share
                piece_out[group, x, l] = rows[at:at + share]
        if tiles == 1:
            for dx, dz in away:
                piece_copy(group, peer_of(line, n_cross, dx), peer_of(me, n_head, dz)).start()
            piece_in[place, head] = piece_out[group, line, me]
        else:
            for dx in range(n_cross):
                x = peer_of(line, n_cross, dx)
                for l in range(sources):
                    z = tile * sources + l
                    if dx:
                        piece_copy(group, x, z).start()
                    else:
                        pl.when(z != me)(piece_copy(group, x, z).start)

                        @pl.when(z == me)
                        def _():
                            piece_in[place, head] = piece_out[group, line, l]

    def step(group, carry):
        compute(group)
        pl.when(group > 0)(lambda: merge(group - 1))
        return carry

    lax.fori_loop(0, groups, step, 0)
    merge(groups - 1)
    for dx, dz in away:
        x, z = peer_of(line, n_cross, dx), peer_of(me, n_head, dz)
        pltpu.make_async_remote_copy(
            src_ref=log_out.at[z // sources, pl.ds(spots - 1 - x * sources - lax.rem(z, sources), 1)],
            dst_ref=log_in.at[pl.ds(place, 1)], send_sem=log_send, recv_sem=log_recv,
            device_id={"head": z, "cache": seat_of(x)}, device_id_type=pl.DeviceIdType.MESH,
        ).start()
    log_in[pl.ds(place, 1)] = log_out[me // sources, pl.ds(spots - 1 - line * sources - lax.rem(me, sources), 1)]
    wait_for(q_all.at[pl.ds(0, n_head - 1), :, width_of(0)], q_send)
    if batches > 1:
        rest = slice(cuts[1] * DH, heads * DH)
        wait_for(q_all.at[pl.ds(0, n_head - 1), rows_of(1, core), rest], q_send)
        wait_for(q_all.at[:, rows_of(1, core), rest], pass_send)
    wait_for(part.at[:, 0], part_send)
    wait_for(piece_in.at[pl.ds(0, others)], piece_send)
    wait_for(piece_in.at[pl.ds(0, others)], piece_recv)
    wait_for(log_in.at[pl.ds(0, others)], log_send)
    wait_for(log_in.at[pl.ds(0, others)], log_recv)
    levels = [log_in[x * n_head:(x + 1) * n_head] for x in range(n_cross)]
    top = functools.reduce(jnp.maximum, levels)
    keeps = [jnp.exp2(level - top) for level in levels]
    total = functools.reduce(jnp.add, keeps)
    inverse = 1.0 / total
    columns = [(keep * inverse).T for keep in keeps]
    logged = (top * LN_2 + jnp.log(total)).T
    lane = lax.broadcasted_iota(jnp.int32, log_ref.shape, 1)
    logs = jnp.zeros(log_ref.shape, jnp.float32)
    for z in range(n_head):
        for head in range(heads):
            column = z * heads + head
            rows = slice(head * share, (head + 1) * share)
            out_ref[:, column * DH:(column + 1) * DH] = functools.reduce(jnp.add, [
                piece_in[x * n_head + z, head] * columns[x][rows, z:z + 1] for x in range(n_cross)
            ])
            logs = jnp.where(lane == column, logged[rows, z:z + 1], logs)
    log_ref[...] = logs


def on_device(queries, keys, values, page_lists, page_counts):
    n_head = lax.axis_size("head")
    n_cache = lax.axis_size("cache")
    tok_local = queries.shape[0]
    heads = keys.shape[2] // DH
    pages = keys.shape[0]
    share = tok_local // n_cache
    sources = TILE // tok_local
    tiles = n_head // sources
    groups = heads * tiles
    n_cross = n_cache // 2
    cuts = tuple(sorted({0, min(1, heads), min(2, heads), min(4, heads), heads}))
    batches = len(cuts) - 1
    plan = (heads, tiles, sources, n_head, n_cache, cuts)
    dma = pltpu.SemaphoreType.DMA
    anywhere = pl.BlockSpec(memory_space=pl.ANY)
    attended, logged = pl.pallas_call(
        functools.partial(kernel, plan),
        out_shape=(
            pltpu.VMEM((share, queries.shape[1]), jnp.float32),
            pltpu.VMEM((share, n_head * heads), jnp.float32),
        ),
        in_specs=[anywhere] * 5,
        out_specs=(pl.BlockSpec(memory_space=pltpu.VMEM), pl.BlockSpec(memory_space=pltpu.VMEM)),
        scratch_shapes=[
            pltpu.VMEM(page_lists.shape, jnp.int32),
            pltpu.SMEM(page_counts.shape, jnp.int32),
            pltpu.VMEM((pages, TILE), jnp.float32),
            pltpu.VMEM((heads, 2, pages, PAGE, DH), jnp.bfloat16),
            pltpu.VMEM((n_head, tok_local, heads * DH), jnp.bfloat16),
            pltpu.VMEM((ROWS, TILE), jnp.float32),
            pltpu.VMEM((2, min(BLOCK, pages), PAGE, TILE), jnp.float32),
            pltpu.VMEM((2 * DH, TILE), jnp.bfloat16),
            pltpu.VMEM((groups, 2, ROWS, LANES), jnp.float32),
            pltpu.VMEM((groups, ROWS, LANES), jnp.float32),
            pltpu.VMEM((groups, n_cross, sources, share, DH), jnp.float32),
            pltpu.VMEM((n_cross * n_head, heads, share, DH), jnp.float32),
            pltpu.VMEM((tiles, n_cross * sources, LANES), jnp.float32),
            pltpu.VMEM((n_cross * n_head, LANES), jnp.float32),
            dma(()),
            dma(()),
            dma((PREFETCH,)),
            dma((2,)),
            dma(()),
            dma((batches,)),
            dma(()),
            dma((batches,)),
            dma(()),
            dma((groups,)),
            dma(()),
            dma(()),
            dma(()),
            dma(()),
        ],
        compiler_params=pltpu.CompilerParams(
            collective_id=0, has_side_effects=True, vmem_limit_bytes=56 * 1024 * 1024
        ),
    )(queries, keys, values, page_lists, page_counts)
    return attended, logged


def solution(mesh):
    in_specs = (
        P(("group", "head"), None),
        P(("group", "cache"), None, "head"),
        P(("group", "cache"), None, "head"),
        P(("group", "cache"), None),
        P(("group", "cache")),
    )
    out_specs = (P(("group", "head", "cache"), None), P(("group", "head", "cache"), None))
    return jax.shard_map(
        on_device, mesh=mesh, in_specs=in_specs, out_specs=out_specs, check_vma=False
    )
```

```python
import functools
import math

import jax
import jax.numpy as jnp
from jax import lax
from jax.experimental import pallas as pl
from jax.experimental.pallas import tpu as pltpu
from jax.sharding import PartitionSpec as P

DH = 128
PAGE = 128
LANES = 128
TILE = 256
ROWS = DH + 8
PAIR = 2
JOIN = 4
BLOCK = 16
PREFETCH = 2
SCALE = 1.0 / math.sqrt(DH)
LOG2_E = math.log2(math.e)
LN_2 = math.log(2.0)
LOG2_SCALE = SCALE * LOG2_E

lowest = -1e30
highest = 3e38


def attend(query, k_ref, v_ref, caps, pages, acc, scores, turned):
    scaled = query * LOG2_SCALE
    high = scaled.astype(jnp.bfloat16)
    low = (scaled - high.astype(jnp.float32)).astype(jnp.bfloat16)
    turned[...] = jnp.concatenate([high, low], axis=1).T
    acc[...] = jnp.zeros_like(acc)
    ones = jnp.ones((16, PAIR * PAGE), jnp.bfloat16)
    block = min(BLOCK, pages)
    blocks = pages // block

    def score(index):
        rows = k_ref[index * block:(index + 1) * block].reshape(block * PAGE, DH)
        scores[index % 2] = jnp.dot(
            jnp.concatenate([rows, rows], axis=1), turned[...], preferred_element_type=jnp.float32
        ).reshape(block, PAGE, TILE)

    def weigh(index, at):
        page = index * block + at
        limits = [caps[page + i:page + i + 1, :] for i in range(PAIR)]
        top = functools.reduce(jnp.maximum, [
            jnp.minimum(jnp.max(scores[index % 2, at + i], axis=0, keepdims=True), limits[i]) for i in range(PAIR)
        ])
        weights = jnp.concatenate([
            jnp.exp2(scores[index % 2, at + i] - jnp.maximum(top, -limits[i])).astype(jnp.bfloat16)
            for i in range(PAIR)
        ], axis=0)
        left = jnp.concatenate([v_ref[page:page + PAIR].reshape(PAIR * PAGE, DH).T, ones], axis=0)
        return top, jnp.dot(left, weights, preferred_element_type=jnp.float32)[:ROWS]

    score(0)
    best = jnp.full((1, TILE), lowest, jnp.float32)
    for index in range(blocks):
        if index + 1 < blocks:
            score(index + 1)
        waiting = []
        for at in range(0, block, PAIR):
            waiting.append(weigh(index, at))
            if len(waiting) == JOIN or at + PAIR >= block:
                running = functools.reduce(jnp.maximum, [top for top, _ in waiting], best)
                joined = acc[...] * jnp.exp2(best - running)
                for top, out in waiting:
                    joined += out * jnp.exp2(top - running)
                acc[...] = joined
                best, waiting = running, []
    return best


def kernel(
    plan, q_hbm, k_hbm, v_hbm, lists_hbm, counts_hbm, out_ref, log_ref,
    lists, counts, caps, kv_buf, q_all, acc, scores, turned, part, part_in, piece_out, piece_in, log_out, log_in,
    lists_sem, counts_sem, kv_sem, own_sem, q_send, q_recv, pass_send, pass_recv,
    part_send, part_recv, piece_send, piece_recv, log_send, log_recv,
):
    heads, tiles, sources, n_head, n_cache, cuts = plan
    batches = len(cuts) - 1
    groups = heads * tiles
    n_cross = n_cache // 2
    others = n_head * n_cross - 1
    spots = n_cross * sources
    pages = k_hbm.shape[0]
    half = q_hbm.shape[0] // 2
    share = q_hbm.shape[0] // n_cache
    me = lax.axis_index("head")
    seat = lax.axis_index("cache")
    core = lax.rem(seat, 2)
    line = seat // 2
    sibling = seat + 1 - 2 * core
    place = line * n_head + me
    away = [(dx, dz) for dx in range(n_cross) for dz in range(n_head) if dx or dz]

    def peer_of(index, count, offset):
        return lax.rem(index + offset, count)

    def seat_of(x):
        return x * 2 + core

    def load(head):
        columns = pl.ds(pl.multiple_of(head * DH, DH), DH)
        sem = kv_sem.at[lax.rem(head, PREFETCH)]
        pltpu.make_async_copy(k_hbm.at[:, :, columns], kv_buf.at[head, 0], sem).start()
        pltpu.make_async_copy(v_hbm.at[:, :, columns], kv_buf.at[head, 1], sem).start()

    def wait_for(ref, sem):
        pltpu.make_async_copy(ref, ref, sem).wait()

    def width_of(batch):
        return slice(cuts[batch] * DH, cuts[batch + 1] * DH)

    def rows_of(batch, side):
        if batch == 0:
            return pl.ds(0, 2 * half)
        return pl.ds(pl.multiple_of(side * half, half), half)

    def query_source(first, last, owner):
        columns = pl.ds(pl.multiple_of((owner * heads + cuts[first]) * DH, DH), (cuts[last] - cuts[first]) * DH)
        return q_hbm.at[rows_of(first, core), columns]

    def own_copy(first, last):
        return pltpu.make_async_copy(
            query_source(first, last, me),
            q_all.at[me, rows_of(first, core), slice(cuts[first] * DH, cuts[last] * DH)], own_sem.at[min(first, 1)],
        )

    def send_queries(batch):
        for offset in range(1, n_head):
            peer = peer_of(me, n_head, offset)
            pltpu.make_async_remote_copy(
                src_ref=query_source(batch, batch + 1, peer),
                dst_ref=q_all.at[me, rows_of(batch, core), width_of(batch)],
                send_sem=q_send, recv_sem=q_recv.at[batch],
                device_id={"head": peer}, device_id_type=pl.DeviceIdType.MESH,
            ).start()

    def pass_copy(batch, side):
        return pltpu.make_async_remote_copy(
            src_ref=q_all.at[:, rows_of(batch, side), width_of(batch)],
            dst_ref=q_all.at[:, rows_of(batch, side), width_of(batch)],
            send_sem=pass_send, recv_sem=pass_recv.at[batch],
            device_id={"cache": sibling}, device_id_type=pl.DeviceIdType.MESH,
        )

    def arrive(batch):
        wait_for(q_all.at[pl.ds(0, n_head - 1), rows_of(batch, 0), width_of(batch)], q_recv.at[batch])

    def hand_on(batch):
        arrive(batch)
        pass_copy(batch, core).start()

    def part_copy(group):
        return pltpu.make_async_remote_copy(
            src_ref=part.at[group, 1 - core], dst_ref=part_in.at[group],
            send_sem=part_send, recv_sem=part_recv.at[group],
            device_id={"cache": sibling}, device_id_type=pl.DeviceIdType.MESH,
        )

    def piece_copy(group, x, z):
        return pltpu.make_async_remote_copy(
            src_ref=piece_out.at[group, x, lax.rem(z, sources)], dst_ref=piece_in.at[place, group // tiles],
            send_sem=piece_send, recv_sem=piece_recv,
            device_id={"head": z, "cache": seat_of(x)}, device_id_type=pl.DeviceIdType.MESH,
        )

    barrier = pltpu.get_barrier_semaphore()
    for dx, dz in away:
        pl.semaphore_signal(
            barrier, inc=1,
            device_id={"head": peer_of(me, n_head, dz), "cache": seat_of(peer_of(line, n_cross, dx))},
            device_id_type=pl.DeviceIdType.MESH,
        )
    pl.semaphore_signal(barrier, inc=1, device_id={"cache": sibling}, device_id_type=pl.DeviceIdType.MESH)
    own_copies = [own_copy(0, 1)] + ([own_copy(1, batches)] if batches > 1 else [])
    for copy in own_copies:
        copy.start()
    lists_copy = pltpu.make_async_copy(lists_hbm, lists, lists_sem)
    counts_copy = pltpu.make_async_copy(counts_hbm, counts, counts_sem)
    lists_copy.start()
    counts_copy.start()
    pl.semaphore_wait(barrier, others + 1)
    for batch in range(min(3, batches)):
        send_queries(batch)
    load(0)
    log_out[...] = jnp.zeros_like(log_out)
    lists_copy.wait()
    counts_copy.wait()
    slots = lists.shape[1]
    used = lax.broadcasted_iota(jnp.int32, (1, slots), 1) < counts[0]
    listed = jnp.where(used, lists[...], -1)
    match = listed == lax.broadcasted_iota(jnp.int32, (pages, slots), 0)
    cap = jnp.max(jnp.where(match, highest, lowest), axis=1, keepdims=True)
    caps[...] = jnp.broadcast_to(cap, caps.shape)
    for copy in own_copies:
        copy.wait()
    for head in range(1, min(PREFETCH, heads)):
        load(head)
    arrive(0)
    for batch in range(3, batches):
        send_queries(batch)
    if batches > 1:
        hand_on(1)

    def only_if(condition, action):
        if isinstance(condition, bool):
            if condition:
                action()
        else:
            pl.when(condition)(action)

    def compute(group):
        head = group // tiles
        tile = lax.rem(group, tiles)

        def ready():
            for batch in range(1, batches):
                pl.when(head == cuts[batch])(lambda: pass_copy(batch, 1 - core).wait_recv())
            wait_for(kv_buf.at[head], kv_sem.at[lax.rem(head, PREFETCH)])
            if heads > PREFETCH:
                pl.when(head + PREFETCH < heads)(lambda: load(head + PREFETCH))
            for batch in range(2, batches):
                pl.when(head == cuts[batch] - 1)(lambda: hand_on(batch))

        only_if(tiles == 1 or tile == 0, ready)
        members = [2 * x + side for side in range(2) for x in range(n_cross)]
        pieces = []
        for member in members:
            for l in range(sources):
                rows = q_all[tile * sources + l, :, pl.ds(pl.multiple_of(head * DH, DH), DH)]
                pieces.append(rows[member * share:(member + 1) * share].astype(jnp.float32))
        query = jnp.concatenate(pieces, axis=0)
        best = attend(query, kv_buf.at[head, 0], kv_buf.at[head, 1], caps, pages, acc, scores, turned)
        row = lax.broadcasted_iota(jnp.int32, (8, TILE), 0)
        tail = jnp.where(row == 1, best, acc[DH:ROWS])
        for side in range(2):
            lanes = slice(side * LANES, (side + 1) * LANES)
            part[group, side, :DH] = acc[:DH, lanes]
            part[group, side, DH:ROWS] = tail[:, lanes]
        part_copy(group).start()

    def merge(group):
        head = group // tiles
        tile = lax.rem(group, tiles)
        part_copy(group).wait_recv()
        totals = [part[group, core, DH:DH + 1], part_in[group, DH:DH + 1]]
        bests = [part[group, core, DH + 1:DH + 2], part_in[group, DH + 1:DH + 2]]
        top = jnp.maximum(*bests)
        keeps = [jnp.exp2(best - top) for best in bests]
        total = totals[0] * keeps[0] + totals[1] * keeps[1]
        inverse = 1.0 / total
        result = part[group, core, :DH] * (keeps[0] * inverse) + part_in[group, :DH] * (keeps[1] * inverse)
        level = jnp.broadcast_to(top + jnp.log(total) * LOG2_E, (spots, LANES))
        level = pltpu.roll(level, 0, 1, stride=share, stride_axis=0)
        level = pltpu.roll(level, lax.rem((head + 1) * share, LANES), 1)
        lane = lax.broadcasted_iota(jnp.int32, (spots, LANES), 1)
        chosen = jnp.logical_and(lane >= head * share, lane < (head + 1) * share)
        log_out[tile] = jnp.where(chosen, level, log_out[tile])
        rows = result.T
        for x in range(n_cross):
            for l in range(sources):
                at = (x * sources + l) * share
                piece_out[group, x, l] = rows[at:at + share]
        if tiles == 1:
            for dx, dz in away:
                piece_copy(group, peer_of(line, n_cross, dx), peer_of(me, n_head, dz)).start()
            piece_in[place, head] = piece_out[group, line, me]
        else:
            for dx in range(n_cross):
                x = peer_of(line, n_cross, dx)
                for l in range(sources):
                    z = tile * sources + l
                    if dx:
                        piece_copy(group, x, z).start()
                    else:
                        pl.when(z != me)(piece_copy(group, x, z).start)

                        @pl.when(z == me)
                        def _():
                            piece_in[place, head] = piece_out[group, line, l]

    def step(group, carry):
        compute(group)
        pl.when(group > 0)(lambda: merge(group - 1))
        return carry

    lax.fori_loop(0, groups, step, 0)
    merge(groups - 1)
    for dx, dz in away:
        x, z = peer_of(line, n_cross, dx), peer_of(me, n_head, dz)
        pltpu.make_async_remote_copy(
            src_ref=log_out.at[z // sources, pl.ds(spots - 1 - x * sources - lax.rem(z, sources), 1)],
            dst_ref=log_in.at[pl.ds(place, 1)], send_sem=log_send, recv_sem=log_recv,
            device_id={"head": z, "cache": seat_of(x)}, device_id_type=pl.DeviceIdType.MESH,
        ).start()
    log_in[pl.ds(place, 1)] = log_out[me // sources, pl.ds(spots - 1 - line * sources - lax.rem(me, sources), 1)]
    wait_for(q_all.at[pl.ds(0, n_head - 1), :, width_of(0)], q_send)
    if batches > 1:
        rest = slice(cuts[1] * DH, heads * DH)
        wait_for(q_all.at[pl.ds(0, n_head - 1), rows_of(1, core), rest], q_send)
        wait_for(q_all.at[:, rows_of(1, core), rest], pass_send)
    wait_for(part.at[:, 0], part_send)
    wait_for(piece_in.at[pl.ds(0, others)], piece_send)
    wait_for(piece_in.at[pl.ds(0, others)], piece_recv)
    wait_for(log_in.at[pl.ds(0, others)], log_send)
    wait_for(log_in.at[pl.ds(0, others)], log_recv)
    levels = [log_in[x * n_head:(x + 1) * n_head] for x in range(n_cross)]
    top = functools.reduce(jnp.maximum, levels)
    keeps = [jnp.exp2(level - top) for level in levels]
    total = functools.reduce(jnp.add, keeps)
    inverse = 1.0 / total
    columns = [(keep * inverse).T for keep in keeps]
    logged = (top * LN_2 + jnp.log(total)).T
    lane = lax.broadcasted_iota(jnp.int32, log_ref.shape, 1)
    logs = jnp.zeros(log_ref.shape, jnp.float32)
    for z in range(n_head):
        for head in range(heads):
            column = z * heads + head
            rows = slice(head * share, (head + 1) * share)
            out_ref[:, column * DH:(column + 1) * DH] = functools.reduce(jnp.add, [
                piece_in[x * n_head + z, head] * columns[x][rows, z:z + 1] for x in range(n_cross)
            ])
            logs = jnp.where(lane == column, logged[rows, z:z + 1], logs)
    log_ref[...] = logs


def store(attended, logged, attended_hbm, logged_hbm, attended_sem, logged_sem):
    copies = (
        pltpu.make_async_copy(attended, attended_hbm, attended_sem),
        pltpu.make_async_copy(logged, logged_hbm, logged_sem),
    )
    for copy in copies:
        copy.start()
    for copy in copies:
        copy.wait()


def on_device(queries, keys, values, page_lists, page_counts):
    n_head = lax.axis_size("head")
    n_cache = lax.axis_size("cache")
    tok_local = queries.shape[0]
    heads = keys.shape[2] // DH
    pages = keys.shape[0]
    share = tok_local // n_cache
    sources = TILE // tok_local
    tiles = n_head // sources
    groups = heads * tiles
    n_cross = n_cache // 2
    cuts = tuple(sorted({0, min(1, heads), min(2, heads), min(4, heads), heads}))
    batches = len(cuts) - 1
    plan = (heads, tiles, sources, n_head, n_cache, cuts)
    dma = pltpu.SemaphoreType.DMA
    anywhere = pl.BlockSpec(memory_space=pl.ANY)
    attended, logged = pl.pallas_call(
        functools.partial(kernel, plan),
        out_shape=(
            pltpu.VMEM((share, queries.shape[1]), jnp.float32),
            pltpu.VMEM((share, n_head * heads), jnp.float32),
        ),
        in_specs=[anywhere] * 5,
        out_specs=(pl.BlockSpec(memory_space=pltpu.VMEM), pl.BlockSpec(memory_space=pltpu.VMEM)),
        scratch_shapes=[
            pltpu.VMEM(page_lists.shape, jnp.int32),
            pltpu.SMEM(page_counts.shape, jnp.int32),
            pltpu.VMEM((pages, TILE), jnp.float32),
            pltpu.VMEM((heads, 2, pages, PAGE, DH), jnp.bfloat16),
            pltpu.VMEM((n_head, tok_local, heads * DH), jnp.bfloat16),
            pltpu.VMEM((ROWS, TILE), jnp.float32),
            pltpu.VMEM((2, min(BLOCK, pages), PAGE, TILE), jnp.float32),
            pltpu.VMEM((2 * DH, TILE), jnp.bfloat16),
            pltpu.VMEM((groups, 2, ROWS, LANES), jnp.float32),
            pltpu.VMEM((groups, ROWS, LANES), jnp.float32),
            pltpu.VMEM((groups, n_cross, sources, share, DH), jnp.float32),
            pltpu.VMEM((n_cross * n_head, heads, share, DH), jnp.float32),
            pltpu.VMEM((tiles, n_cross * sources, LANES), jnp.float32),
            pltpu.VMEM((n_cross * n_head, LANES), jnp.float32),
            dma(()),
            dma(()),
            dma((PREFETCH,)),
            dma((2,)),
            dma(()),
            dma((batches,)),
            dma(()),
            dma((batches,)),
            dma(()),
            dma((groups,)),
            dma(()),
            dma(()),
            dma(()),
            dma(()),
        ],
        compiler_params=pltpu.CompilerParams(
            collective_id=0, has_side_effects=True, vmem_limit_bytes=56 * 1024 * 1024
        ),
    )(queries, keys, values, page_lists, page_counts)
    return pl.pallas_call(
        store,
        out_shape=(
            jax.ShapeDtypeStruct(attended.shape, jnp.float32), jax.ShapeDtypeStruct(logged.shape, jnp.float32)
        ),
        in_specs=[pl.BlockSpec(memory_space=pltpu.VMEM)] * 2,
        out_specs=(anywhere, anywhere),
        scratch_shapes=[dma(()), dma(())],
    )(pltpu.with_memory_space_constraint(attended, pltpu.VMEM), pltpu.with_memory_space_constraint(logged, pltpu.VMEM))


def solution(mesh):
    in_specs = (
        P(("group", "head"), None),
        P(("group", "cache"), None, "head"),
        P(("group", "cache"), None, "head"),
        P(("group", "cache"), None),
        P(("group", "cache")),
    )
    out_specs = (P(("group", "head", "cache"), None), P(("group", "head", "cache"), None))
    return jax.shard_map(
        on_device, mesh=mesh, in_specs=in_specs, out_specs=out_specs, check_vma=False
    )
```

```python
import functools
import math

import jax
import jax.numpy as jnp
from jax import lax
from jax.experimental import pallas as pl
from jax.experimental.pallas import tpu as pltpu
from jax.sharding import PartitionSpec as P

DH = 128
PAGE = 128
LANES = 128
TILE = 256
ROWS = DH + 8
PAIR = 2
JOIN = 4
PREFETCH = 2
SCALE = 1.0 / math.sqrt(DH)
LOG2_E = math.log2(math.e)
LN_2 = math.log(2.0)
LOG2_SCALE = SCALE * LOG2_E

lowest = -1e30
highest = 3e38


def attend(query, k_ref, v_ref, caps, pages, acc, scores, turned):
    scaled = query * LOG2_SCALE
    high = scaled.astype(jnp.bfloat16)
    low = (scaled - high.astype(jnp.float32)).astype(jnp.bfloat16)
    turned[...] = jnp.concatenate([high, low], axis=1).T
    ones = jnp.ones((16, PAIR * PAGE), jnp.bfloat16)
    cut = pages * 3 // 16 * 2
    blocks = [(0, cut), (cut, pages)]

    def score(first, last):
        rows = k_ref[first:last].reshape((last - first) * PAGE, DH)
        scores[first:last] = jnp.dot(
            jnp.concatenate([rows, rows], axis=1), turned[...], preferred_element_type=jnp.float32
        ).reshape(last - first, PAGE, TILE)

    def weigh(page):
        limits = [caps[page + i:page + i + 1, :] for i in range(PAIR)]
        top = functools.reduce(jnp.maximum, [
            jnp.minimum(jnp.max(scores[page + i], axis=0, keepdims=True), limits[i]) for i in range(PAIR)
        ])
        weights = jnp.concatenate([
            jnp.exp2(scores[page + i] - jnp.maximum(top, -limits[i])).astype(jnp.bfloat16) for i in range(PAIR)
        ], axis=0)
        left = jnp.concatenate([v_ref[page:page + PAIR].reshape(PAIR * PAGE, DH).T, ones], axis=0)
        return top, jnp.dot(left, weights, preferred_element_type=jnp.float32)[:ROWS]

    score(*blocks[0])
    best = jnp.full((1, TILE), lowest, jnp.float32)
    started = False
    for index, (first, last) in enumerate(blocks):
        if index + 1 < len(blocks):
            score(*blocks[index + 1])
        waiting = []
        for page in range(first, last, PAIR):
            waiting.append(weigh(page))
            if len(waiting) == JOIN or page + PAIR >= last:
                running = functools.reduce(jnp.maximum, [top for top, _ in waiting], best)
                joined = functools.reduce(jnp.add, [out * jnp.exp2(top - running) for top, out in waiting])
                if started:
                    joined += jnp.concatenate([acc[0], acc[1]], axis=1) * jnp.exp2(best - running)
                acc[0] = joined[:, :LANES]
                acc[1] = joined[:, LANES:]
                best, waiting, started = running, [], True
    return best


def kernel(
    plan, q_hbm, k_hbm, v_hbm, lists_hbm, counts_hbm, out_ref, log_ref,
    lists, counts, caps, kv_buf, q_all, scores, turned, part, part_in, piece_out, piece_in, log_out, log_in,
    lists_sem, counts_sem, kv_sem, own_sem, q_send, q_recv, pass_send, pass_recv,
    part_send, part_recv, piece_send, piece_recv, log_send, log_recv,
):
    heads, tiles, sources, n_head, n_cache, cuts = plan
    batches = len(cuts) - 1
    groups = heads * tiles
    n_cross = n_cache // 2
    others = n_head * n_cross - 1
    spots = n_cross * sources
    pages = k_hbm.shape[0]
    half = q_hbm.shape[0] // 2
    share = q_hbm.shape[0] // n_cache
    me = lax.axis_index("head")
    seat = lax.axis_index("cache")
    core = lax.rem(seat, 2)
    line = seat // 2
    sibling = seat + 1 - 2 * core
    place = line * n_head + me
    upper = me // (n_head // 2)
    away = [(dx, dz) for dz in [*range(1, n_head), 0] for dx in reversed(range(n_cross)) if dx or dz]

    def peer_of(index, count, offset):
        return lax.rem(index + offset, count)

    def far_first(rank):
        return lax.rem(me + n_head - rank + upper * (2 * rank - n_head) + n_head, n_head) if rank else me

    def seat_of(x):
        return x * 2 + core

    def load(head):
        columns = pl.ds(pl.multiple_of(head * DH, DH), DH)
        sem = kv_sem.at[lax.rem(head, PREFETCH)]
        pltpu.make_async_copy(k_hbm.at[:, :, columns], kv_buf.at[head, 0], sem).start()
        pltpu.make_async_copy(v_hbm.at[:, :, columns], kv_buf.at[head, 1], sem).start()

    def wait_for(ref, sem):
        pltpu.make_async_copy(ref, ref, sem).wait()

    def width_of(batch):
        return slice(cuts[batch] * DH, cuts[batch + 1] * DH)

    def rows_of(batch, side):
        if batch == 0:
            return pl.ds(0, 2 * half)
        return pl.ds(pl.multiple_of(side * half, half), half)

    def query_source(first, last, owner):
        columns = pl.ds(pl.multiple_of((owner * heads + cuts[first]) * DH, DH), (cuts[last] - cuts[first]) * DH)
        return q_hbm.at[rows_of(first, core), columns]

    def own_copy(first, last):
        return pltpu.make_async_copy(
            query_source(first, last, me),
            q_all.at[me, rows_of(first, core), slice(cuts[first] * DH, cuts[last] * DH)], own_sem.at[min(first, 1)],
        )

    def send_queries(batch):
        for rank in range(1, n_head):
            peer = far_first(rank)
            pltpu.make_async_remote_copy(
                src_ref=query_source(batch, batch + 1, peer),
                dst_ref=q_all.at[me, rows_of(batch, core), width_of(batch)],
                send_sem=q_send, recv_sem=q_recv.at[batch],
                device_id={"head": peer}, device_id_type=pl.DeviceIdType.MESH,
            ).start()

    def pass_copy(batch, side):
        return pltpu.make_async_remote_copy(
            src_ref=q_all.at[:, rows_of(batch, side), width_of(batch)],
            dst_ref=q_all.at[:, rows_of(batch, side), width_of(batch)],
            send_sem=pass_send, recv_sem=pass_recv.at[batch],
            device_id={"cache": sibling}, device_id_type=pl.DeviceIdType.MESH,
        )

    def arrive(batch):
        wait_for(q_all.at[pl.ds(0, n_head - 1), rows_of(batch, 0), width_of(batch)], q_recv.at[batch])

    def hand_on(batch):
        arrive(batch)
        pass_copy(batch, core).start()

    def part_copy(group):
        return pltpu.make_async_remote_copy(
            src_ref=part.at[group, 1 - core], dst_ref=part_in.at[group],
            send_sem=part_send, recv_sem=part_recv.at[group],
            device_id={"cache": sibling}, device_id_type=pl.DeviceIdType.MESH,
        )

    def piece_copy(group, x, z):
        return pltpu.make_async_remote_copy(
            src_ref=piece_out.at[group, x, lax.rem(z, sources)], dst_ref=piece_in.at[place, group // tiles],
            send_sem=piece_send, recv_sem=piece_recv,
            device_id={"head": z, "cache": seat_of(x)}, device_id_type=pl.DeviceIdType.MESH,
        )

    barrier = pltpu.get_barrier_semaphore()
    for dx, dz in away:
        pl.semaphore_signal(
            barrier, inc=1,
            device_id={"head": far_first(dz), "cache": seat_of(peer_of(line, n_cross, dx))},
            device_id_type=pl.DeviceIdType.MESH,
        )
    pl.semaphore_signal(barrier, inc=1, device_id={"cache": sibling}, device_id_type=pl.DeviceIdType.MESH)
    own_copies = [own_copy(0, 1)] + ([own_copy(1, batches)] if batches > 1 else [])
    for copy in own_copies:
        copy.start()
    lists_copy = pltpu.make_async_copy(lists_hbm, lists, lists_sem)
    counts_copy = pltpu.make_async_copy(counts_hbm, counts, counts_sem)
    lists_copy.start()
    counts_copy.start()
    pl.semaphore_wait(barrier, others + 1)
    for batch in range(min(3, batches)):
        send_queries(batch)
    load(0)
    log_out[...] = jnp.zeros_like(log_out)
    lists_copy.wait()
    counts_copy.wait()
    slots = lists.shape[1]
    used = lax.broadcasted_iota(jnp.int32, (1, slots), 1) < counts[0]
    listed = jnp.where(used, lists[...], -1)
    match = listed == lax.broadcasted_iota(jnp.int32, (pages, slots), 0)
    cap = jnp.max(jnp.where(match, highest, lowest), axis=1, keepdims=True)
    caps[...] = jnp.broadcast_to(cap, caps.shape)
    for copy in own_copies:
        copy.wait()
    for head in range(1, min(PREFETCH, heads)):
        load(head)
    arrive(0)
    for batch in range(3, batches):
        send_queries(batch)
    if batches > 1:
        hand_on(1)

    def only_if(condition, action):
        if isinstance(condition, bool):
            if condition:
                action()
        else:
            pl.when(condition)(action)

    def compute(group):
        head = group // tiles
        tile = lax.rem(group, tiles)

        def ready():
            for batch in range(1, batches):
                pl.when(head == cuts[batch])(lambda: pass_copy(batch, 1 - core).wait_recv())
            wait_for(kv_buf.at[head], kv_sem.at[lax.rem(head, PREFETCH)])
            if heads > PREFETCH:
                pl.when(head + PREFETCH < heads)(lambda: load(head + PREFETCH))
            for batch in range(2, batches):
                pl.when(head == cuts[batch] - 1)(lambda: hand_on(batch))

        only_if(tiles == 1 or tile == 0, ready)
        members = [2 * x + side for side in range(2) for x in range(n_cross)]
        pieces = []
        for member in members:
            for l in range(sources):
                rows = q_all[tile * sources + l, :, pl.ds(pl.multiple_of(head * DH, DH), DH)]
                pieces.append(rows[member * share:(member + 1) * share].astype(jnp.float32))
        query = jnp.concatenate(pieces, axis=0)
        best = attend(query, kv_buf.at[head, 0], kv_buf.at[head, 1], caps, pages, part.at[group], scores, turned)
        for side in range(2):
            part[group, side, DH + 1:DH + 2] = best[:, side * LANES:(side + 1) * LANES]
        part_copy(group).start()

    def merge(group):
        head = group // tiles
        tile = lax.rem(group, tiles)
        part_copy(group).wait_recv()
        totals = [part[group, core, DH:DH + 1], part_in[group, DH:DH + 1]]
        bests = [part[group, core, DH + 1:DH + 2], part_in[group, DH + 1:DH + 2]]
        top = jnp.maximum(*bests)
        keeps = [jnp.exp2(best - top) for best in bests]
        total = totals[0] * keeps[0] + totals[1] * keeps[1]
        inverse = 1.0 / total
        result = part[group, core, :DH] * (keeps[0] * inverse) + part_in[group, :DH] * (keeps[1] * inverse)
        level = jnp.broadcast_to(top + jnp.log(total) * LOG2_E, (spots, LANES))
        level = pltpu.roll(level, 0, 1, stride=share, stride_axis=0)
        level = pltpu.roll(level, lax.rem((head + 1) * share, LANES), 1)
        lane = lax.broadcasted_iota(jnp.int32, (spots, LANES), 1)
        chosen = jnp.logical_and(lane >= head * share, lane < (head + 1) * share)
        log_out[tile] = jnp.where(chosen, level, log_out[tile])
        rows = result.T
        for x in range(n_cross):
            for l in range(sources):
                at = (x * sources + l) * share
                piece_out[group, x, l] = rows[at:at + share]
        if tiles == 1:
            for dx, dz in away:
                piece_copy(group, peer_of(line, n_cross, dx), far_first(dz)).start()
            piece_in[place, head] = piece_out[group, line, me]
        else:
            for dx in range(n_cross):
                x = peer_of(line, n_cross, dx)
                for l in range(sources):
                    z = tile * sources + l
                    if dx:
                        piece_copy(group, x, z).start()
                    else:
                        pl.when(z != me)(piece_copy(group, x, z).start)

                        @pl.when(z == me)
                        def _():
                            piece_in[place, head] = piece_out[group, line, l]

    def step(group, carry):
        compute(group)
        pl.when(group > 0)(lambda: merge(group - 1))
        return carry

    lax.fori_loop(0, groups, step, 0)
    merge(groups - 1)
    for dx, dz in away:
        x, z = peer_of(line, n_cross, dx), far_first(dz)
        pltpu.make_async_remote_copy(
            src_ref=log_out.at[z // sources, pl.ds(spots - 1 - x * sources - lax.rem(z, sources), 1)],
            dst_ref=log_in.at[pl.ds(place, 1)], send_sem=log_send, recv_sem=log_recv,
            device_id={"head": z, "cache": seat_of(x)}, device_id_type=pl.DeviceIdType.MESH,
        ).start()
    log_in[pl.ds(place, 1)] = log_out[me // sources, pl.ds(spots - 1 - line * sources - lax.rem(me, sources), 1)]
    wait_for(q_all.at[pl.ds(0, n_head - 1), :, width_of(0)], q_send)
    if batches > 1:
        rest = slice(cuts[1] * DH, heads * DH)
        wait_for(q_all.at[pl.ds(0, n_head - 1), rows_of(1, core), rest], q_send)
        wait_for(q_all.at[:, rows_of(1, core), rest], pass_send)
    wait_for(part.at[:, 0], part_send)
    wait_for(piece_in.at[pl.ds(0, others)], piece_send)
    wait_for(piece_in.at[pl.ds(0, others)], piece_recv)
    wait_for(log_in.at[pl.ds(0, others)], log_send)
    wait_for(log_in.at[pl.ds(0, others)], log_recv)
    levels = [log_in[x * n_head:(x + 1) * n_head] for x in range(n_cross)]
    top = functools.reduce(jnp.maximum, levels)
    keeps = [jnp.exp2(level - top) for level in levels]
    total = functools.reduce(jnp.add, keeps)
    inverse = 1.0 / total
    columns = [(keep * inverse).T for keep in keeps]
    logged = (top * LN_2 + jnp.log(total)).T
    lane = lax.broadcasted_iota(jnp.int32, log_ref.shape, 1)
    logs = jnp.zeros(log_ref.shape, jnp.float32)
    for z in range(n_head):
        for head in range(heads):
            column = z * heads + head
            rows = slice(head * share, (head + 1) * share)
            out_ref[:, column * DH:(column + 1) * DH] = functools.reduce(jnp.add, [
                piece_in[x * n_head + z, head] * columns[x][rows, z:z + 1] for x in range(n_cross)
            ])
            logs = jnp.where(lane == column, logged[rows, z:z + 1], logs)
    log_ref[...] = logs


def store(attended, logged, attended_hbm, logged_hbm, attended_sem, logged_sem):
    copies = (
        pltpu.make_async_copy(attended, attended_hbm, attended_sem),
        pltpu.make_async_copy(logged, logged_hbm, logged_sem),
    )
    for copy in copies:
        copy.start()
    for copy in copies:
        copy.wait()


def on_device(queries, keys, values, page_lists, page_counts):
    n_head = lax.axis_size("head")
    n_cache = lax.axis_size("cache")
    tok_local = queries.shape[0]
    heads = keys.shape[2] // DH
    pages = keys.shape[0]
    share = tok_local // n_cache
    sources = TILE // tok_local
    tiles = n_head // sources
    groups = heads * tiles
    n_cross = n_cache // 2
    cuts = tuple(sorted({0, min(1, heads), min(2, heads), min(4, heads), heads}))
    batches = len(cuts) - 1
    plan = (heads, tiles, sources, n_head, n_cache, cuts)
    dma = pltpu.SemaphoreType.DMA
    anywhere = pl.BlockSpec(memory_space=pl.ANY)
    attended, logged = pl.pallas_call(
        functools.partial(kernel, plan),
        out_shape=(
            pltpu.VMEM((share, queries.shape[1]), jnp.float32),
            pltpu.VMEM((share, n_head * heads), jnp.float32),
        ),
        in_specs=[anywhere] * 5,
        out_specs=(pl.BlockSpec(memory_space=pltpu.VMEM), pl.BlockSpec(memory_space=pltpu.VMEM)),
        scratch_shapes=[
            pltpu.VMEM(page_lists.shape, jnp.int32),
            pltpu.SMEM(page_counts.shape, jnp.int32),
            pltpu.VMEM((pages, TILE), jnp.float32),
            pltpu.VMEM((heads, 2, pages, PAGE, DH), jnp.bfloat16),
            pltpu.VMEM((n_head, tok_local, heads * DH), jnp.bfloat16),
            pltpu.VMEM((pages, PAGE, TILE), jnp.float32),
            pltpu.VMEM((2 * DH, TILE), jnp.bfloat16),
            pltpu.VMEM((groups, 2, ROWS, LANES), jnp.float32),
            pltpu.VMEM((groups, ROWS, LANES), jnp.float32),
            pltpu.VMEM((groups, n_cross, sources, share, DH), jnp.float32),
            pltpu.VMEM((n_cross * n_head, heads, share, DH), jnp.float32),
            pltpu.VMEM((tiles, n_cross * sources, LANES), jnp.float32),
            pltpu.VMEM((n_cross * n_head, LANES), jnp.float32),
            dma(()),
            dma(()),
            dma((PREFETCH,)),
            dma((2,)),
            dma(()),
            dma((batches,)),
            dma(()),
            dma((batches,)),
            dma(()),
            dma((groups,)),
            dma(()),
            dma(()),
            dma(()),
            dma(()),
        ],
        compiler_params=pltpu.CompilerParams(
            collective_id=0, has_side_effects=True, vmem_limit_bytes=56 * 1024 * 1024
        ),
    )(queries, keys, values, page_lists, page_counts)
    return pl.pallas_call(
        store,
        out_shape=(
            jax.ShapeDtypeStruct(attended.shape, jnp.float32), jax.ShapeDtypeStruct(logged.shape, jnp.float32)
        ),
        in_specs=[pl.BlockSpec(memory_space=pltpu.VMEM)] * 2,
        out_specs=(anywhere, anywhere),
        scratch_shapes=[dma(()), dma(())],
    )(pltpu.with_memory_space_constraint(attended, pltpu.VMEM), pltpu.with_memory_space_constraint(logged, pltpu.VMEM))


def solution(mesh):
    in_specs = (
        P(("group", "head"), None),
        P(("group", "cache"), None, "head"),
        P(("group", "cache"), None, "head"),
        P(("group", "cache"), None),
        P(("group", "cache")),
    )
    out_specs = (P(("group", "head", "cache"), None), P(("group", "head", "cache"), None))
    return jax.shard_map(
        on_device, mesh=mesh, in_specs=in_specs, out_specs=out_specs, check_vma=False
    )
```

```python
import functools
import math

import jax
import jax.numpy as jnp
from jax import lax
from jax.experimental import pallas as pl
from jax.experimental.pallas import tpu as pltpu
from jax.sharding import PartitionSpec as P

DH = 128
PAGE = 128
LANES = 128
TILE = 256
ROWS = DH + 8
PAIR = 2
JOIN = 8
PREFETCH = 2
SCALE = 1.0 / math.sqrt(DH)
LOG2_E = math.log2(math.e)
LN_2 = math.log(2.0)
LOG2_SCALE = SCALE * LOG2_E

lowest = -1e30
highest = 3e38


def attend(query, k_ref, v_ref, caps, pages, acc, scores, turned):
    scaled = query * LOG2_SCALE
    high = scaled.astype(jnp.bfloat16)
    low = (scaled - high.astype(jnp.float32)).astype(jnp.bfloat16)
    turned[...] = jnp.concatenate([high, low], axis=1).T
    ones = jnp.ones((16, PAIR * PAGE), jnp.bfloat16)
    cut = pages * 3 // 16 * 2
    blocks = [(0, cut), (cut, pages)]

    def score(first, last):
        rows = k_ref[first:last].reshape((last - first) * PAGE, DH)
        scores[first:last] = jnp.dot(
            jnp.concatenate([rows, rows], axis=1), turned[...], preferred_element_type=jnp.float32
        ).reshape(last - first, PAGE, TILE)

    def weigh(page):
        limits = [caps[page + i:page + i + 1, :] for i in range(PAIR)]
        top = functools.reduce(jnp.maximum, [
            jnp.minimum(jnp.max(scores[page + i], axis=0, keepdims=True), limits[i]) for i in range(PAIR)
        ])
        weights = jnp.concatenate([
            jnp.exp2(scores[page + i] - jnp.maximum(top, -limits[i])).astype(jnp.bfloat16) for i in range(PAIR)
        ], axis=0)
        left = jnp.concatenate([v_ref[page:page + PAIR].reshape(PAIR * PAGE, DH).T, ones], axis=0)
        return top, jnp.dot(left, weights, preferred_element_type=jnp.float32)[:ROWS]

    score(*blocks[0])
    best = jnp.full((1, TILE), lowest, jnp.float32)
    started = False
    for index, (first, last) in enumerate(blocks):
        if index + 1 < len(blocks):
            score(*blocks[index + 1])
        waiting = []
        for page in range(first, last, PAIR):
            waiting.append(weigh(page))
            if len(waiting) == JOIN or page + PAIR >= last:
                running = functools.reduce(jnp.maximum, [top for top, _ in waiting], best)
                joined = functools.reduce(jnp.add, [out * jnp.exp2(top - running) for top, out in waiting])
                if started:
                    joined += jnp.concatenate([acc[0], acc[1]], axis=1) * jnp.exp2(best - running)
                acc[0] = joined[:, :LANES]
                acc[1] = joined[:, LANES:]
                best, waiting, started = running, [], True
    return best


def kernel(
    plan, q_hbm, k_hbm, v_hbm, lists_hbm, counts_hbm, piece_in, log_in,
    lists, counts, caps, kv_buf, q_all, scores, turned, part, part_in, piece_out, log_out,
    lists_sem, counts_sem, kv_sem, own_sem, q_send, q_recv, pass_send, pass_recv,
    part_send, part_recv, piece_send, piece_recv, log_send, log_recv,
):
    heads, tiles, sources, n_head, n_cache, cuts = plan
    batches = len(cuts) - 1
    groups = heads * tiles
    n_cross = n_cache // 2
    others = n_head * n_cross - 1
    spots = n_cross * sources
    pages = k_hbm.shape[0]
    half = q_hbm.shape[0] // 2
    share = q_hbm.shape[0] // n_cache
    me = lax.axis_index("head")
    seat = lax.axis_index("cache")
    core = lax.rem(seat, 2)
    line = seat // 2
    sibling = seat + 1 - 2 * core
    place = line * n_head + me
    upper = me // (n_head // 2)
    away = [(dx, dz) for dz in [*range(1, n_head), 0] for dx in reversed(range(n_cross)) if dx or dz]

    def peer_of(index, count, offset):
        return lax.rem(index + offset, count)

    def far_first(rank):
        return lax.rem(me + n_head - rank + upper * (2 * rank - n_head) + n_head, n_head) if rank else me

    def seat_of(x):
        return x * 2 + core

    def load(head):
        columns = pl.ds(pl.multiple_of(head * DH, DH), DH)
        sem = kv_sem.at[lax.rem(head, PREFETCH)]
        pltpu.make_async_copy(k_hbm.at[:, :, columns], kv_buf.at[head, 0], sem).start()
        pltpu.make_async_copy(v_hbm.at[:, :, columns], kv_buf.at[head, 1], sem).start()

    def wait_for(ref, sem):
        pltpu.make_async_copy(ref, ref, sem).wait()

    def width_of(batch):
        return slice(cuts[batch] * DH, cuts[batch + 1] * DH)

    def rows_of(batch, side):
        if batch == 0:
            return pl.ds(0, 2 * half)
        return pl.ds(pl.multiple_of(side * half, half), half)

    def query_source(first, last, owner):
        columns = pl.ds(pl.multiple_of((owner * heads + cuts[first]) * DH, DH), (cuts[last] - cuts[first]) * DH)
        return q_hbm.at[rows_of(first, core), columns]

    def own_copy(first, last):
        return pltpu.make_async_copy(
            query_source(first, last, me),
            q_all.at[me, rows_of(first, core), slice(cuts[first] * DH, cuts[last] * DH)], own_sem.at[min(first, 1)],
        )

    def send_queries(batch):
        for rank in range(1, n_head):
            peer = far_first(rank)
            pltpu.make_async_remote_copy(
                src_ref=query_source(batch, batch + 1, peer),
                dst_ref=q_all.at[me, rows_of(batch, core), width_of(batch)],
                send_sem=q_send, recv_sem=q_recv.at[batch],
                device_id={"head": peer}, device_id_type=pl.DeviceIdType.MESH,
            ).start()

    def pass_copy(batch, side):
        return pltpu.make_async_remote_copy(
            src_ref=q_all.at[:, rows_of(batch, side), width_of(batch)],
            dst_ref=q_all.at[:, rows_of(batch, side), width_of(batch)],
            send_sem=pass_send, recv_sem=pass_recv.at[batch],
            device_id={"cache": sibling}, device_id_type=pl.DeviceIdType.MESH,
        )

    def arrive(batch):
        wait_for(q_all.at[pl.ds(0, n_head - 1), rows_of(batch, 0), width_of(batch)], q_recv.at[batch])

    def hand_on(batch):
        arrive(batch)
        pass_copy(batch, core).start()

    def part_copy(group):
        return pltpu.make_async_remote_copy(
            src_ref=part.at[group, 1 - core], dst_ref=part_in.at[group],
            send_sem=part_send, recv_sem=part_recv.at[group],
            device_id={"cache": sibling}, device_id_type=pl.DeviceIdType.MESH,
        )

    def piece_copy(group, x, z):
        return pltpu.make_async_remote_copy(
            src_ref=piece_out.at[group, x, lax.rem(z, sources)], dst_ref=piece_in.at[place, group // tiles],
            send_sem=piece_send, recv_sem=piece_recv,
            device_id={"head": z, "cache": seat_of(x)}, device_id_type=pl.DeviceIdType.MESH,
        )

    barrier = pltpu.get_barrier_semaphore()
    for dx, dz in away:
        pl.semaphore_signal(
            barrier, inc=1,
            device_id={"head": far_first(dz), "cache": seat_of(peer_of(line, n_cross, dx))},
            device_id_type=pl.DeviceIdType.MESH,
        )
    pl.semaphore_signal(barrier, inc=1, device_id={"cache": sibling}, device_id_type=pl.DeviceIdType.MESH)
    own_copies = [own_copy(0, 1)] + ([own_copy(1, batches)] if batches > 1 else [])
    for copy in own_copies:
        copy.start()
    lists_copy = pltpu.make_async_copy(lists_hbm, lists, lists_sem)
    counts_copy = pltpu.make_async_copy(counts_hbm, counts, counts_sem)
    lists_copy.start()
    counts_copy.start()
    pl.semaphore_wait(barrier, others + 1)
    for batch in range(min(3, batches)):
        send_queries(batch)
    load(0)
    log_out[...] = jnp.zeros_like(log_out)
    lists_copy.wait()
    counts_copy.wait()
    slots = lists.shape[1]
    used = lax.broadcasted_iota(jnp.int32, (1, slots), 1) < counts[0]
    listed = jnp.where(used, lists[...], -1)
    match = listed == lax.broadcasted_iota(jnp.int32, (pages, slots), 0)
    cap = jnp.max(jnp.where(match, highest, lowest), axis=1, keepdims=True)
    caps[...] = jnp.broadcast_to(cap, caps.shape)
    for copy in own_copies:
        copy.wait()
    for head in range(1, min(PREFETCH, heads)):
        load(head)
    arrive(0)
    for batch in range(3, batches):
        send_queries(batch)
    if batches > 1:
        hand_on(1)

    def only_if(condition, action):
        if isinstance(condition, bool):
            if condition:
                action()
        else:
            pl.when(condition)(action)

    def compute(group):
        head = group // tiles
        tile = lax.rem(group, tiles)

        def ready():
            for batch in range(1, batches):
                pl.when(head == cuts[batch])(lambda: pass_copy(batch, 1 - core).wait_recv())
            wait_for(kv_buf.at[head], kv_sem.at[lax.rem(head, PREFETCH)])
            if heads > PREFETCH:
                pl.when(head + PREFETCH < heads)(lambda: load(head + PREFETCH))
            for batch in range(2, batches):
                pl.when(head == cuts[batch] - 1)(lambda: hand_on(batch))

        only_if(tiles == 1 or tile == 0, ready)
        members = [2 * x + side for side in range(2) for x in range(n_cross)]
        pieces = []
        for member in members:
            for l in range(sources):
                rows = q_all[tile * sources + l, :, pl.ds(pl.multiple_of(head * DH, DH), DH)]
                pieces.append(rows[member * share:(member + 1) * share].astype(jnp.float32))
        query = jnp.concatenate(pieces, axis=0)
        best = attend(query, kv_buf.at[head, 0], kv_buf.at[head, 1], caps, pages, part.at[group], scores, turned)
        for side in range(2):
            part[group, side, DH + 1:DH + 2] = best[:, side * LANES:(side + 1) * LANES]
        part_copy(group).start()

    def merge(group):
        head = group // tiles
        tile = lax.rem(group, tiles)
        part_copy(group).wait_recv()
        totals = [part[group, core, DH:DH + 1], part_in[group, DH:DH + 1]]
        bests = [part[group, core, DH + 1:DH + 2], part_in[group, DH + 1:DH + 2]]
        top = jnp.maximum(*bests)
        keeps = [jnp.exp2(best - top) for best in bests]
        total = totals[0] * keeps[0] + totals[1] * keeps[1]
        inverse = 1.0 / total
        result = part[group, core, :DH] * (keeps[0] * inverse) + part_in[group, :DH] * (keeps[1] * inverse)
        level = jnp.broadcast_to(top + jnp.log(total) * LOG2_E, (spots, LANES))
        level = pltpu.roll(level, 0, 1, stride=share, stride_axis=0)
        level = pltpu.roll(level, lax.rem((head + 1) * share, LANES), 1)
        lane = lax.broadcasted_iota(jnp.int32, (spots, LANES), 1)
        chosen = jnp.logical_and(lane >= head * share, lane < (head + 1) * share)
        log_out[tile] = jnp.where(chosen, level, log_out[tile])
        rows = result.T
        for x in range(n_cross):
            for l in range(sources):
                at = (x * sources + l) * share
                piece_out[group, x, l] = rows[at:at + share]
        if tiles == 1:
            for dx, dz in away:
                piece_copy(group, peer_of(line, n_cross, dx), far_first(dz)).start()
            piece_in[place, head] = piece_out[group, line, me]
        else:
            for dx in range(n_cross):
                x = peer_of(line, n_cross, dx)
                for l in range(sources):
                    z = tile * sources + l
                    if dx:
                        piece_copy(group, x, z).start()
                    else:
                        pl.when(z != me)(piece_copy(group, x, z).start)

                        @pl.when(z == me)
                        def _():
                            piece_in[place, head] = piece_out[group, line, l]

    def step(group, carry):
        compute(group)
        pl.when(group > 0)(lambda: merge(group - 1))
        return carry

    lax.fori_loop(0, groups, step, 0)
    merge(groups - 1)
    for dx, dz in away:
        x, z = peer_of(line, n_cross, dx), far_first(dz)
        pltpu.make_async_remote_copy(
            src_ref=log_out.at[z // sources, pl.ds(spots - 1 - x * sources - lax.rem(z, sources), 1)],
            dst_ref=log_in.at[pl.ds(place, 1)], send_sem=log_send, recv_sem=log_recv,
            device_id={"head": z, "cache": seat_of(x)}, device_id_type=pl.DeviceIdType.MESH,
        ).start()
    log_in[pl.ds(place, 1)] = log_out[me // sources, pl.ds(spots - 1 - line * sources - lax.rem(me, sources), 1)]
    wait_for(q_all.at[pl.ds(0, n_head - 1), :, width_of(0)], q_send)
    if batches > 1:
        rest = slice(cuts[1] * DH, heads * DH)
        wait_for(q_all.at[pl.ds(0, n_head - 1), rows_of(1, core), rest], q_send)
        wait_for(q_all.at[:, rows_of(1, core), rest], pass_send)
    wait_for(part.at[:, 0], part_send)
    wait_for(piece_in.at[pl.ds(0, others)], piece_send)
    wait_for(piece_in.at[pl.ds(0, others)], piece_recv)
    wait_for(log_in.at[pl.ds(0, others)], log_send)
    wait_for(log_in.at[pl.ds(0, others)], log_recv)


def combine(plan, piece_in, log_in, attended_hbm, logged_hbm, attended, logged, attended_sem, logged_sem):
    heads, _, _, n_head, n_cache, _ = plan
    n_cross = n_cache // 2
    share = attended.shape[0]
    width = heads * DH
    levels = [log_in[x * n_head:(x + 1) * n_head] for x in range(n_cross)]
    top = functools.reduce(jnp.maximum, levels)
    keeps = [jnp.exp2(level - top) for level in levels]
    total = functools.reduce(jnp.add, keeps)
    inverse = 1.0 / total
    columns = [(keep * inverse).T for keep in keeps]
    values = (top * LN_2 + jnp.log(total)).T
    lane = lax.broadcasted_iota(jnp.int32, logged.shape, 1)
    logs = jnp.zeros(logged.shape, jnp.float32)
    for z in range(n_head):
        for head in range(heads):
            rows = slice(head * share, (head + 1) * share)
            logs = jnp.where(lane == z * heads + head, values[rows, z:z + 1], logs)
    logged[...] = logs
    logged_copy = pltpu.make_async_copy(logged, logged_hbm, logged_sem)
    logged_copy.start()
    for z in range(n_head):
        for head in range(heads):
            at = z * width + head * DH
            rows = slice(head * share, (head + 1) * share)
            attended[:, at:at + DH] = functools.reduce(jnp.add, [
                piece_in[x * n_head + z, head] * columns[x][rows, z:z + 1] for x in range(n_cross)
            ])
        block = slice(z * width, (z + 1) * width)
        pltpu.make_async_copy(attended.at[:, block], attended_hbm.at[:, block], attended_sem).start()
    pltpu.make_async_copy(attended, attended_hbm, attended_sem).wait()
    logged_copy.wait()


def on_device(queries, keys, values, page_lists, page_counts):
    n_head = lax.axis_size("head")
    n_cache = lax.axis_size("cache")
    tok_local = queries.shape[0]
    heads = keys.shape[2] // DH
    pages = keys.shape[0]
    share = tok_local // n_cache
    sources = TILE // tok_local
    tiles = n_head // sources
    groups = heads * tiles
    n_cross = n_cache // 2
    cuts = tuple(sorted({0, min(1, heads), min(2, heads), min(3, heads), min(5, heads), heads}))
    batches = len(cuts) - 1
    plan = (heads, tiles, sources, n_head, n_cache, cuts)
    dma = pltpu.SemaphoreType.DMA
    anywhere = pl.BlockSpec(memory_space=pl.ANY)
    pieces, logs = pl.pallas_call(
        functools.partial(kernel, plan),
        out_shape=(
            pltpu.VMEM((n_cross * n_head, heads, share, DH), jnp.float32),
            pltpu.VMEM((n_cross * n_head, LANES), jnp.float32),
        ),
        in_specs=[anywhere] * 5,
        out_specs=(pl.BlockSpec(memory_space=pltpu.VMEM), pl.BlockSpec(memory_space=pltpu.VMEM)),
        scratch_shapes=[
            pltpu.VMEM(page_lists.shape, jnp.int32),
            pltpu.SMEM(page_counts.shape, jnp.int32),
            pltpu.VMEM((pages, TILE), jnp.float32),
            pltpu.VMEM((heads, 2, pages, PAGE, DH), jnp.bfloat16),
            pltpu.VMEM((n_head, tok_local, heads * DH), jnp.bfloat16),
            pltpu.VMEM((pages, PAGE, TILE), jnp.float32),
            pltpu.VMEM((2 * DH, TILE), jnp.bfloat16),
            pltpu.VMEM((groups, 2, ROWS, LANES), jnp.float32),
            pltpu.VMEM((groups, ROWS, LANES), jnp.float32),
            pltpu.VMEM((groups, n_cross, sources, share, DH), jnp.float32),
            pltpu.VMEM((tiles, n_cross * sources, LANES), jnp.float32),
            dma(()),
            dma(()),
            dma((PREFETCH,)),
            dma((2,)),
            dma(()),
            dma((batches,)),
            dma(()),
            dma((batches,)),
            dma(()),
            dma((groups,)),
            dma(()),
            dma(()),
            dma(()),
            dma(()),
        ],
        compiler_params=pltpu.CompilerParams(
            collective_id=0, has_side_effects=True, vmem_limit_bytes=56 * 1024 * 1024
        ),
    )(queries, keys, values, page_lists, page_counts)
    attended = jax.ShapeDtypeStruct((share, queries.shape[1]), jnp.float32)
    logged = jax.ShapeDtypeStruct((share, n_head * heads), jnp.float32)
    return pl.pallas_call(
        functools.partial(combine, plan),
        out_shape=(attended, logged),
        in_specs=[pl.BlockSpec(memory_space=pltpu.VMEM)] * 2,
        out_specs=(anywhere, anywhere),
        scratch_shapes=[
            pltpu.VMEM(attended.shape, jnp.float32), pltpu.VMEM(logged.shape, jnp.float32), dma(()), dma(())
        ],
    )(pltpu.with_memory_space_constraint(pieces, pltpu.VMEM), pltpu.with_memory_space_constraint(logs, pltpu.VMEM))


def solution(mesh):
    in_specs = (
        P(("group", "head"), None),
        P(("group", "cache"), None, "head"),
        P(("group", "cache"), None, "head"),
        P(("group", "cache"), None),
        P(("group", "cache")),
    )
    out_specs = (P(("group", "head", "cache"), None), P(("group", "head", "cache"), None))
    return jax.shard_map(
        on_device, mesh=mesh, in_specs=in_specs, out_specs=out_specs, check_vma=False
    )
```

```python
import functools
import math

import jax
import jax.numpy as jnp
from jax import lax
from jax.experimental import pallas as pl
from jax.experimental.pallas import tpu as pltpu
from jax.sharding import PartitionSpec as P

DH = 128
PAGE = 128
LANES = 128
TILE = 256
ROWS = DH + 8
PAIR = 2
JOIN = 8
PREFETCH = 2
SCALE = 1.0 / math.sqrt(DH)
LOG2_E = math.log2(math.e)
LN_2 = math.log(2.0)
LOG2_SCALE = SCALE * LOG2_E

lowest = -1e30
highest = 3e38


def attend(query, k_ref, v_ref, caps, pages, acc, scores, turned):
    scaled = query * LOG2_SCALE
    high = scaled.astype(jnp.bfloat16)
    low = (scaled - high.astype(jnp.float32)).astype(jnp.bfloat16)
    turned[...] = jnp.concatenate([high, low], axis=1).T
    ones = jnp.ones((16, PAIR * PAGE), jnp.bfloat16)
    cut = pages * 3 // 16 * 2
    blocks = [(0, cut), (cut, pages)]

    def score(first, last):
        rows = k_ref[first:last].reshape((last - first) * PAGE, DH)
        scores[first:last] = jnp.dot(
            jnp.concatenate([rows, rows], axis=1), turned[...], preferred_element_type=jnp.float32
        ).reshape(last - first, PAGE, TILE)

    def weigh(page):
        limits = [caps[page + i:page + i + 1, :] for i in range(PAIR)]
        top = functools.reduce(jnp.maximum, [
            jnp.minimum(jnp.max(scores[page + i], axis=0, keepdims=True), limits[i]) for i in range(PAIR)
        ])
        weights = jnp.concatenate([
            jnp.exp2(scores[page + i] - jnp.maximum(top, -limits[i])).astype(jnp.bfloat16) for i in range(PAIR)
        ], axis=0)
        left = jnp.concatenate([v_ref[page:page + PAIR].reshape(PAIR * PAGE, DH).T, ones], axis=0)
        return top, jnp.dot(left, weights, preferred_element_type=jnp.float32)[:ROWS]

    score(*blocks[0])
    best = jnp.full((1, TILE), lowest, jnp.float32)
    started = False
    for index, (first, last) in enumerate(blocks):
        if index + 1 < len(blocks):
            score(*blocks[index + 1])
        waiting = []
        for page in range(first, last, PAIR):
            waiting.append(weigh(page))
            if len(waiting) == JOIN or page + PAIR >= last:
                running = functools.reduce(jnp.maximum, [top for top, _ in waiting], best)
                joined = functools.reduce(jnp.add, [out * jnp.exp2(top - running) for top, out in waiting])
                if started:
                    joined += jnp.concatenate([acc[0], acc[1]], axis=1) * jnp.exp2(best - running)
                acc[0] = joined[:, :LANES]
                acc[1] = joined[:, LANES:]
                best, waiting, started = running, [], True
    return best


def kernel(
    plan, q_hbm, k_hbm, v_hbm, lists_hbm, counts_hbm, piece_in, log_in,
    lists, counts, caps, kv_buf, q_all, scores, turned, part, part_in, piece_out, log_out,
    lists_sem, counts_sem, kv_sem, own_sem, q_send, q_recv, pass_send, pass_recv,
    part_send, part_recv, piece_send, piece_recv, log_send, log_recv,
):
    heads, tiles, sources, n_head, n_cache, cuts = plan
    batches = len(cuts) - 1
    groups = heads * tiles
    n_cross = n_cache // 2
    others = n_head * n_cross - 1
    spots = n_cross * sources
    pages = k_hbm.shape[0]
    half = q_hbm.shape[0] // 2
    share = q_hbm.shape[0] // n_cache
    me = lax.axis_index("head")
    seat = lax.axis_index("cache")
    core = lax.rem(seat, 2)
    line = seat // 2
    sibling = seat + 1 - 2 * core
    place = line * n_head + me
    upper = me // (n_head // 2)
    away = [(dx, dz) for dz in [*range(1, n_head), 0] for dx in reversed(range(n_cross)) if dx or dz]

    def peer_of(index, count, offset):
        return lax.rem(index + offset, count)

    def far_first(rank):
        return lax.rem(me + n_head - rank + upper * (2 * rank - n_head) + n_head, n_head) if rank else me

    def seat_of(x):
        return x * 2 + core

    def load(head):
        columns = pl.ds(pl.multiple_of(head * DH, DH), DH)
        sem = kv_sem.at[lax.rem(head, PREFETCH)]
        pltpu.make_async_copy(k_hbm.at[:, :, columns], kv_buf.at[head, 0], sem).start()
        pltpu.make_async_copy(v_hbm.at[:, :, columns], kv_buf.at[head, 1], sem).start()

    def wait_for(ref, sem):
        pltpu.make_async_copy(ref, ref, sem).wait()

    def width_of(batch):
        return slice(cuts[batch] * DH, cuts[batch + 1] * DH)

    def rows_of(batch, side):
        if batch == 0:
            return pl.ds(0, 2 * half)
        return pl.ds(pl.multiple_of(side * half, half), half)

    def query_source(first, last, owner):
        columns = pl.ds(pl.multiple_of((owner * heads + cuts[first]) * DH, DH), (cuts[last] - cuts[first]) * DH)
        return q_hbm.at[rows_of(first, core), columns]

    def own_copy(first, last):
        return pltpu.make_async_copy(
            query_source(first, last, me),
            q_all.at[me, rows_of(first, core), slice(cuts[first] * DH, cuts[last] * DH)], own_sem.at[min(first, 1)],
        )

    def send_queries(batch):
        for rank in range(1, n_head):
            peer = far_first(rank)
            pltpu.make_async_remote_copy(
                src_ref=query_source(batch, batch + 1, peer),
                dst_ref=q_all.at[me, rows_of(batch, core), width_of(batch)],
                send_sem=q_send, recv_sem=q_recv.at[batch],
                device_id={"head": peer}, device_id_type=pl.DeviceIdType.MESH,
            ).start()

    def pass_copy(batch, side):
        return pltpu.make_async_remote_copy(
            src_ref=q_all.at[:, rows_of(batch, side), width_of(batch)],
            dst_ref=q_all.at[:, rows_of(batch, side), width_of(batch)],
            send_sem=pass_send, recv_sem=pass_recv.at[batch],
            device_id={"cache": sibling}, device_id_type=pl.DeviceIdType.MESH,
        )

    def arrive(batch):
        wait_for(q_all.at[pl.ds(0, n_head - 1), rows_of(batch, 0), width_of(batch)], q_recv.at[batch])

    def hand_on(batch):
        arrive(batch)
        pass_copy(batch, core).start()

    def part_copy(group):
        return pltpu.make_async_remote_copy(
            src_ref=part.at[group, 1 - core], dst_ref=part_in.at[group],
            send_sem=part_send, recv_sem=part_recv.at[group],
            device_id={"cache": sibling}, device_id_type=pl.DeviceIdType.MESH,
        )

    def piece_copy(group, x, z):
        return pltpu.make_async_remote_copy(
            src_ref=piece_out.at[group, x, lax.rem(z, sources)], dst_ref=piece_in.at[place, group // tiles],
            send_sem=piece_send, recv_sem=piece_recv,
            device_id={"head": z, "cache": seat_of(x)}, device_id_type=pl.DeviceIdType.MESH,
        )

    barrier = pltpu.get_barrier_semaphore()
    for dx, dz in away:
        pl.semaphore_signal(
            barrier, inc=1,
            device_id={"head": far_first(dz), "cache": seat_of(peer_of(line, n_cross, dx))},
            device_id_type=pl.DeviceIdType.MESH,
        )
    pl.semaphore_signal(barrier, inc=1, device_id={"cache": sibling}, device_id_type=pl.DeviceIdType.MESH)
    own_copies = [own_copy(0, 1)] + ([own_copy(1, batches)] if batches > 1 else [])
    for copy in own_copies:
        copy.start()
    lists_copy = pltpu.make_async_copy(lists_hbm, lists, lists_sem)
    counts_copy = pltpu.make_async_copy(counts_hbm, counts, counts_sem)
    lists_copy.start()
    counts_copy.start()
    load(0)
    pl.semaphore_wait(barrier, others + 1)
    for batch in range(min(3, batches)):
        send_queries(batch)
    log_out[...] = jnp.zeros_like(log_out)
    lists_copy.wait()
    counts_copy.wait()
    slots = lists.shape[1]
    used = lax.broadcasted_iota(jnp.int32, (1, slots), 1) < counts[0]
    listed = jnp.where(used, lists[...], -1)
    match = listed == lax.broadcasted_iota(jnp.int32, (pages, slots), 0)
    cap = jnp.max(jnp.where(match, highest, lowest), axis=1, keepdims=True)
    caps[...] = jnp.broadcast_to(cap, caps.shape)
    for copy in own_copies:
        copy.wait()
    arrive(0)
    for head in range(1, min(PREFETCH, heads)):
        load(head)
    for batch in range(3, batches):
        send_queries(batch)
    if batches > 1:
        hand_on(1)

    def only_if(condition, action):
        if isinstance(condition, bool):
            if condition:
                action()
        else:
            pl.when(condition)(action)

    def compute(group):
        head = group // tiles
        tile = lax.rem(group, tiles)

        def ready():
            for batch in range(1, batches):
                pl.when(head == cuts[batch])(lambda: pass_copy(batch, 1 - core).wait_recv())
            wait_for(kv_buf.at[head], kv_sem.at[lax.rem(head, PREFETCH)])
            if heads > PREFETCH:
                pl.when(head + PREFETCH < heads)(lambda: load(head + PREFETCH))
            for batch in range(2, batches):
                pl.when(head == cuts[batch] - 1)(lambda: hand_on(batch))

        only_if(tiles == 1 or tile == 0, ready)
        members = [2 * x + side for side in range(2) for x in range(n_cross)]
        pieces = []
        for member in members:
            for l in range(sources):
                rows = q_all[tile * sources + l, :, pl.ds(pl.multiple_of(head * DH, DH), DH)]
                pieces.append(rows[member * share:(member + 1) * share].astype(jnp.float32))
        query = jnp.concatenate(pieces, axis=0)
        best = attend(query, kv_buf.at[head, 0], kv_buf.at[head, 1], caps, pages, part.at[group], scores, turned)
        for side in range(2):
            part[group, side, DH + 1:DH + 2] = best[:, side * LANES:(side + 1) * LANES]
        part_copy(group).start()

    def merge(group):
        head = group // tiles
        tile = lax.rem(group, tiles)
        part_copy(group).wait_recv()
        totals = [part[group, core, DH:DH + 1], part_in[group, DH:DH + 1]]
        bests = [part[group, core, DH + 1:DH + 2], part_in[group, DH + 1:DH + 2]]
        top = jnp.maximum(*bests)
        keeps = [jnp.exp2(best - top) for best in bests]
        total = totals[0] * keeps[0] + totals[1] * keeps[1]
        inverse = 1.0 / total
        result = part[group, core, :DH] * (keeps[0] * inverse) + part_in[group, :DH] * (keeps[1] * inverse)
        level = jnp.broadcast_to(top + jnp.log(total) * LOG2_E, (spots, LANES))
        level = pltpu.roll(level, 0, 1, stride=share, stride_axis=0)
        level = pltpu.roll(level, lax.rem((head + 1) * share, LANES), 1)
        lane = lax.broadcasted_iota(jnp.int32, (spots, LANES), 1)
        chosen = jnp.logical_and(lane >= head * share, lane < (head + 1) * share)
        log_out[tile] = jnp.where(chosen, level, log_out[tile])
        rows = result.T
        for x in range(n_cross):
            for l in range(sources):
                at = (x * sources + l) * share
                piece_out[group, x, l] = rows[at:at + share]
        if tiles == 1:
            for dx, dz in away:
                piece_copy(group, peer_of(line, n_cross, dx), far_first(dz)).start()
            piece_in[place, head] = piece_out[group, line, me]
        else:
            for dx in range(n_cross):
                x = peer_of(line, n_cross, dx)
                for l in range(sources):
                    z = tile * sources + l
                    if dx:
                        piece_copy(group, x, z).start()
                    else:
                        pl.when(z != me)(piece_copy(group, x, z).start)

                        @pl.when(z == me)
                        def _():
                            piece_in[place, head] = piece_out[group, line, l]

    def step(group, carry):
        compute(group)
        pl.when(group > 0)(lambda: merge(group - 1))
        return carry

    lax.fori_loop(0, groups, step, 0)
    merge(groups - 1)
    for dx, dz in away:
        x, z = peer_of(line, n_cross, dx), far_first(dz)
        pltpu.make_async_remote_copy(
            src_ref=log_out.at[z // sources, pl.ds(spots - 1 - x * sources - lax.rem(z, sources), 1)],
            dst_ref=log_in.at[pl.ds(place, 1)], send_sem=log_send, recv_sem=log_recv,
            device_id={"head": z, "cache": seat_of(x)}, device_id_type=pl.DeviceIdType.MESH,
        ).start()
    log_in[pl.ds(place, 1)] = log_out[me // sources, pl.ds(spots - 1 - line * sources - lax.rem(me, sources), 1)]
    wait_for(q_all.at[pl.ds(0, n_head - 1), :, width_of(0)], q_send)
    if batches > 1:
        rest = slice(cuts[1] * DH, heads * DH)
        wait_for(q_all.at[pl.ds(0, n_head - 1), rows_of(1, core), rest], q_send)
        wait_for(q_all.at[:, rows_of(1, core), rest], pass_send)
    wait_for(part.at[:, 0], part_send)
    wait_for(piece_in.at[pl.ds(0, others)], piece_send)
    wait_for(piece_in.at[pl.ds(0, others)], piece_recv)
    wait_for(log_in.at[pl.ds(0, others)], log_send)
    wait_for(log_in.at[pl.ds(0, others)], log_recv)


def combine(plan, piece_in, log_in, attended_hbm, logged_hbm, attended, logged, attended_sem, logged_sem):
    heads, _, _, n_head, n_cache, _ = plan
    n_cross = n_cache // 2
    share = attended.shape[0]
    width = heads * DH
    levels = [log_in[x * n_head:(x + 1) * n_head] for x in range(n_cross)]
    top = functools.reduce(jnp.maximum, levels)
    keeps = [jnp.exp2(level - top) for level in levels]
    total = functools.reduce(jnp.add, keeps)
    inverse = 1.0 / total
    columns = [(keep * inverse).T for keep in keeps]
    values = (top * LN_2 + jnp.log(total)).T
    lane = lax.broadcasted_iota(jnp.int32, logged.shape, 1)
    logs = jnp.zeros(logged.shape, jnp.float32)
    for z in range(n_head):
        for head in range(heads):
            rows = slice(head * share, (head + 1) * share)
            logs = jnp.where(lane == z * heads + head, values[rows, z:z + 1], logs)
    logged[...] = logs
    logged_copy = pltpu.make_async_copy(logged, logged_hbm, logged_sem)
    logged_copy.start()
    for z in range(n_head):
        for head in range(heads):
            at = z * width + head * DH
            rows = slice(head * share, (head + 1) * share)
            attended[:, at:at + DH] = functools.reduce(jnp.add, [
                piece_in[x * n_head + z, head] * columns[x][rows, z:z + 1] for x in range(n_cross)
            ])
        block = slice(z * width, (z + 1) * width)
        pltpu.make_async_copy(attended.at[:, block], attended_hbm.at[:, block], attended_sem).start()
    pltpu.make_async_copy(attended, attended_hbm, attended_sem).wait()
    logged_copy.wait()


def on_device(queries, keys, values, page_lists, page_counts):
    n_head = lax.axis_size("head")
    n_cache = lax.axis_size("cache")
    tok_local = queries.shape[0]
    heads = keys.shape[2] // DH
    pages = keys.shape[0]
    share = tok_local // n_cache
    sources = TILE // tok_local
    tiles = n_head // sources
    groups = heads * tiles
    n_cross = n_cache // 2
    cuts = tuple(sorted({0, min(1, heads), min(2, heads), min(3, heads), min(5, heads), heads}))
    batches = len(cuts) - 1
    plan = (heads, tiles, sources, n_head, n_cache, cuts)
    dma = pltpu.SemaphoreType.DMA
    anywhere = pl.BlockSpec(memory_space=pl.ANY)
    pieces, logs = pl.pallas_call(
        functools.partial(kernel, plan),
        out_shape=(
            pltpu.VMEM((n_cross * n_head, heads, share, DH), jnp.float32),
            pltpu.VMEM((n_cross * n_head, LANES), jnp.float32),
        ),
        in_specs=[anywhere] * 5,
        out_specs=(pl.BlockSpec(memory_space=pltpu.VMEM), pl.BlockSpec(memory_space=pltpu.VMEM)),
        scratch_shapes=[
            pltpu.VMEM(page_lists.shape, jnp.int32),
            pltpu.SMEM(page_counts.shape, jnp.int32),
            pltpu.VMEM((pages, TILE), jnp.float32),
            pltpu.VMEM((heads, 2, pages, PAGE, DH), jnp.bfloat16),
            pltpu.VMEM((n_head, tok_local, heads * DH), jnp.bfloat16),
            pltpu.VMEM((pages, PAGE, TILE), jnp.float32),
            pltpu.VMEM((2 * DH, TILE), jnp.bfloat16),
            pltpu.VMEM((groups, 2, ROWS, LANES), jnp.float32),
            pltpu.VMEM((groups, ROWS, LANES), jnp.float32),
            pltpu.VMEM((groups, n_cross, sources, share, DH), jnp.float32),
            pltpu.VMEM((tiles, n_cross * sources, LANES), jnp.float32),
            dma(()),
            dma(()),
            dma((PREFETCH,)),
            dma((2,)),
            dma(()),
            dma((batches,)),
            dma(()),
            dma((batches,)),
            dma(()),
            dma((groups,)),
            dma(()),
            dma(()),
            dma(()),
            dma(()),
        ],
        compiler_params=pltpu.CompilerParams(
            collective_id=0, has_side_effects=True, vmem_limit_bytes=56 * 1024 * 1024
        ),
    )(queries, keys, values, page_lists, page_counts)
    attended = jax.ShapeDtypeStruct((share, queries.shape[1]), jnp.float32)
    logged = jax.ShapeDtypeStruct((share, n_head * heads), jnp.float32)
    return pl.pallas_call(
        functools.partial(combine, plan),
        out_shape=(attended, logged),
        in_specs=[pl.BlockSpec(memory_space=pltpu.VMEM)] * 2,
        out_specs=(anywhere, anywhere),
        scratch_shapes=[
            pltpu.VMEM(attended.shape, jnp.float32), pltpu.VMEM(logged.shape, jnp.float32), dma(()), dma(())
        ],
    )(pltpu.with_memory_space_constraint(pieces, pltpu.VMEM), pltpu.with_memory_space_constraint(logs, pltpu.VMEM))


def solution(mesh):
    in_specs = (
        P(("group", "head"), None),
        P(("group", "cache"), None, "head"),
        P(("group", "cache"), None, "head"),
        P(("group", "cache"), None),
        P(("group", "cache")),
    )
    out_specs = (P(("group", "head", "cache"), None), P(("group", "head", "cache"), None))
    return jax.shard_map(
        on_device, mesh=mesh, in_specs=in_specs, out_specs=out_specs, check_vma=False
    )
```
